256 devices in a mesh: ch: 32 (over z_lo, y, core), ta: 8 (over z_hi, x).
Axes of the slice: x: 4, y: 4, z: 8 (z_hi: 2, z_lo: 4; z = z_hi * 4 + z_lo), core: 2. Of those that a mesh axis runs over, the one named last changes fastest.
Arguments:
- templates: bfloat16 [64, 200, 8192], P('ta', None, 'ch')
- record: float32 [8192, 2048], P('ch', 'ta')
- record_tail: float32 [8192, 199], P('ch')
Outputs:
- stacked: float32 [64, 2048], P('ch', 'ta')
All inputs are finite; a program needn't handle non-finite values.
Results may differ from the reference program's by a relative error of at most 0.00044.
Values may be sent and summed in bfloat16 or wider, within the bound.
No kernel may reach another device: no remote copies, remote signals or barrier semaphores. Data moves between devices by JAX's collectives and lax.ppermute only.
A program may use at most 128 MiB of HBM per device.

```python
import math
import jax
import jax.numpy as jnp
from jax import lax

C = 8192
M = 200
K = 64
LAGS = 2048


def make_scene(key):
    base = jax.random.fold_in(key, 7301)
    keys = jax.random.split(base, 9)
    raw = jax.random.normal(keys[0], (K, M, C), jnp.float32)
    noise = jax.random.normal(keys[4], (C, LAGS + M - 1), jnp.float32)
    t_scale = jnp.exp(jax.random.uniform(keys[1], (K, 1, C), jnp.float32, jnp.log(0.3), jnp.log(3.0)))
    t_shift = jax.random.uniform(keys[2], (K, 1, C), jnp.float32, -1.0, 1.0)
    templ = ((raw + t_shift) * t_scale).astype(jnp.bfloat16).astype(jnp.float32)
    c_scale = jnp.exp(jax.random.uniform(keys[5], (C, 1), jnp.float32, jnp.log(0.2), jnp.log(2.0)))
    c_shift = jax.random.uniform(keys[8], (C, 1), jnp.float32, -1.0, 1.0)
    signal = noise * c_scale + c_shift
    onsets = jax.random.randint(keys[6], (K * 4,), 0, LAGS).astype(jnp.int32)
    amounts = jax.random.uniform(keys[7], (K * 4,), jnp.float32, 0.5, 2.0)

    def plant(event, current):
        which = event // 4
        piece = jnp.transpose(lax.dynamic_index_in_dim(templ, which, 0, False)) * amounts[event]
        anchor = (jnp.int32(0), onsets[event])
        present = lax.dynamic_slice(current, anchor, (C, M))
        return lax.dynamic_update_slice(current, present + piece, anchor)
    signal = lax.fori_loop(0, K * 4, plant, signal)
    return (templ.astype(jnp.bfloat16), signal)


def draw_templates(key, part):
    return make_scene(key)[0]


def draw_record(key, part):
    return make_scene(key)[1][:, :LAGS]


def draw_record_tail(key, part):
    return make_scene(key)[1][:, LAGS:]


def setup_inputs(seed: int = 0) -> dict:
    seeds = jax.random.split(jax.random.key(seed), 4)
    return {
        "templates": draw_templates(jax.random.fold_in(seeds[3], 71), 0),
        "record": draw_record(jax.random.fold_in(seeds[3], 71), 0),
        "record_tail": draw_record_tail(jax.random.fold_in(seeds[3], 71), 0),
    }


def reference(templates, record, record_tail):
    samples = templates.shape[1]
    channels = templates.shape[2]
    lag_count = record.shape[1]
    values = templates.astype(jnp.float32)
    centred = values - lax.optimization_barrier(jnp.mean(values, axis=1, keepdims=True))
    normed = (centred * lax.rsqrt(lax.optimization_barrier(jnp.mean(centred * centred, axis=1, keepdims=True)) + 1e-06) / math.sqrt(samples)).astype(jnp.bfloat16)
    full_trace = jnp.concatenate([record, record_tail], axis=1)
    block_rows = math.gcd(channels, 32)
    block_count = channels // block_rows

    def advance(running, block_index):
        first_row = (block_index * block_rows).astype(jnp.int32)
        channel_rows = lax.dynamic_slice_in_dim(full_trace, first_row, block_rows, 0)
        hankel = jnp.stack([channel_rows[:, offset:offset + lag_count] for offset in range(samples)], axis=1)
        window_mean = lax.optimization_barrier(jnp.mean(hankel, axis=1, keepdims=True))
        deviation = hankel - window_mean
        window_var = lax.optimization_barrier(jnp.mean(deviation * deviation, axis=1, keepdims=True))
        windows = (deviation * lax.rsqrt(window_var + 1e-06) / math.sqrt(samples)).astype(jnp.bfloat16)
        unit_part = lax.dynamic_slice_in_dim(normed, first_row, block_rows, 2)
        running = running + jnp.einsum('kmc,cmt->kt', unit_part.astype(jnp.float32), windows.astype(jnp.float32))
        return (running, None)
    running, unused = lax.scan(advance, jnp.zeros((templates.shape[0], lag_count), jnp.float32), jnp.arange(block_count, dtype=jnp.int32))
    return running / channels
```

```python
import functools
import math

import jax
import jax.numpy as jnp
from jax import lax
from jax.experimental import pallas as pl
from jax.experimental.pallas import tpu as pltpu
from jax.sharding import PartitionSpec as P

C = 8192
M = 200
K_LOC = 8
B = 16
CB = 32
SLAB = 256
TA = 8
LANES = 128
TILES = 16


def toeplitz_kernel(t_ref, out_ref, sum_ref, ut):
    sub = pl.program_id(1)

    @pl.when(sub == 0)
    def _():
        for k in range(K_LOC):
            v = t_ref[k].astype(jnp.float32)
            v = v - jnp.sum(v, axis=0, keepdims=True) / M
            var = jnp.sum(v * v, axis=0, keepdims=True) / M
            unit = (v * lax.rsqrt(var + 1e-6) / math.sqrt(M)).astype(jnp.bfloat16).astype(jnp.float32)
            sum_ref[k : k + 1, :] = jnp.sum(unit, axis=0, keepdims=True)
            padded = jnp.concatenate([unit, jnp.zeros((256 - M, LANES), jnp.float32)], axis=0)
            ut[k] = padded.T

    def group(g, carry):
        base = sub * CB + g * 8
        for cc in range(8):
            for k in range(K_LOC):
                row = jnp.broadcast_to(ut[k, pl.ds(base + cc, 1), :], (8, 256))
                low = pltpu.roll(row, 0, 1, stride=1, stride_axis=0)
                high = pltpu.roll(row, 8, 1, stride=1, stride_axis=0)
                both = jnp.concatenate([low, high], axis=0)
                out_ref[g * 8 + cc, B * k : B * k + B, :] = both.astype(jnp.bfloat16)
        return carry

    lax.fori_loop(0, CB // 8, group, 0)


def toeplitz(templates):
    c_loc = templates.shape[2]
    return pl.pallas_call(
        toeplitz_kernel,
        grid=(c_loc // LANES, LANES // CB),
        in_specs=[pl.BlockSpec((K_LOC, M, LANES), lambda h, s: (0, 0, h))],
        out_specs=[
            pl.BlockSpec((CB, K_LOC * B, 256), lambda h, s: (h * (LANES // CB) + s, 0, 0)),
            pl.BlockSpec((K_LOC, LANES), lambda h, s: (0, h)),
        ],
        out_shape=[
            jax.ShapeDtypeStruct((c_loc, K_LOC * B, 256), jnp.bfloat16),
            jax.ShapeDtypeStruct((K_LOC, c_loc), jnp.float32),
        ],
        scratch_shapes=[pltpu.VMEM((K_LOC, LANES, 256), jnp.float32)],
        cost_estimate=pl.CostEstimate(flops=10**9, bytes_accessed=18 * 10**6, transcendentals=0),
        name="toeplitz",
    )(templates)


def correlate_kernel(order, *refs):
    slabs = refs[:TA]
    tail_ref, toep_ref, usum_ref, out_ref = refs[TA : TA + 4]
    xa, xb, s_scr, mu_s, band, acc, d_scr, rolled = refs[TA + 4 :]
    step = pl.program_id(0)
    f32, bf16 = jnp.float32, jnp.bfloat16

    @pl.when(step == 0)
    def _():
        j = lax.broadcasted_iota(jnp.int32, (512, 256), 0)
        t = lax.broadcasted_iota(jnp.int32, (512, 256), 1)
        band[...] = jnp.where((j >= t) & (j < t + M), 1.0, 0.0).astype(bf16)
        acc[...] = jnp.zeros_like(acc)

    for i in range(TA):
        where = pl.ds(pl.multiple_of(order[i] * SLAB, SLAB), SLAB)
        part = slabs[i][...]
        xb[:, where] = part
        xa[:, :, where] = part.astype(f32).reshape(CB // 8, 8, SLAB)
    xb[:, TA * SLAB :] = tail_ref[...]
    xa[:, :, TA * SLAB :] = tail_ref[...].astype(f32).reshape(CB // 8, 8, SLAB)

    firsts, highs, lows, centres = [], [], [], []
    for b in range(TA):
        window = xa[:, :, SLAB * b : SLAB * b + 512].reshape(CB, 512)
        centre = jnp.mean(window, axis=1, keepdims=True)
        y = window - centre
        y2 = y * y
        high = y2.astype(bf16)
        firsts.append(xb[:, SLAB * b : SLAB * b + 512])
        highs.append(high)
        lows.append((y2 - high.astype(f32)).astype(bf16))
        centres.append(centre)
    dot = functools.partial(jnp.dot, preferred_element_type=f32)
    bandv = band[...]
    s1 = dot(jnp.concatenate(firsts, axis=0), bandv) * (1.0 / M)
    s2 = dot(jnp.concatenate(highs, axis=0), bandv) + dot(jnp.concatenate(lows, axis=0), bandv)
    s2 = s2 * (1.0 / M)
    for b in range(TA):
        mean = s1[CB * b : CB * b + CB]
        near = mean - centres[b]
        var = jnp.maximum(s2[CB * b : CB * b + CB] - near * near, 0.0)
        scale = lax.rsqrt(var + 1e-6) * (1.0 / math.sqrt(M))
        s_scr[:, :, SLAB * b : SLAB * b + SLAB] = scale.reshape(CB // 8, 8, SLAB)
        mu_s[pl.ds(pl.multiple_of(step * CB, CB), CB), SLAB * b : SLAB * b + SLAB] = (mean * scale).astype(bf16)

    lane = lax.broadcasted_iota(jnp.int32, (8, LANES), 1)
    back = 7 - lax.broadcasted_iota(jnp.int32, (8, LANES), 0)
    inside = lane + B * back < LANES
    pick = B * back + lane % B

    def group(g, carry):
        for cc in range(8):
            c = g * 8 + cc
            turned = []
            for q in range(TILES + 2):
                row = jnp.broadcast_to(xa[g, cc : cc + 1, LANES * q : LANES * q + LANES], (8, LANES))
                turned.append(pltpu.roll(row, B, 1, stride=B, stride_axis=0))
            tiles = [jnp.where(inside, turned[q], turned[q + 1]) for q in range(TILES + 1)]
            x0 = jnp.concatenate(tiles[:TILES], axis=0).astype(bf16)
            x1 = jnp.concatenate(tiles[1:], axis=0).astype(bf16)
            x = jnp.concatenate([x0, x1], axis=1)
            prod = lax.dot_general(
                x, toep_ref[c], (((1,), (1,)), ((), ())), preferred_element_type=f32
            )
            scales = []
            for q in range(TILES):
                row = jnp.broadcast_to(s_scr[g, cc : cc + 1, LANES * q : LANES * q + LANES], (8, LANES))
                scales.append(jnp.take_along_axis(row, pick, axis=1))
            acc[...] += prod * jnp.concatenate(scales, axis=0)
        return carry

    lax.fori_loop(0, CB // 8, group, 0)

    @pl.when(step == pl.num_programs(0) - 1)
    def _():
        usum = usum_ref[...]
        uh = usum.astype(bf16)
        ul = (usum - uh.astype(f32)).astype(bf16)
        smu = mu_s[...]
        d_scr[...] = dot(uh, smu) + dot(ul, smu)
        for q in range(TILES):
            fix = jnp.zeros((8, LANES), f32)
            for k in range(K_LOC):
                row = jnp.broadcast_to(d_scr[k : k + 1, LANES * q : LANES * q + LANES], (8, LANES))
                fix = jnp.where(lane // B == k, jnp.take_along_axis(row, pick, axis=1), fix)
            acc[8 * q : 8 * q + 8, :] -= fix
        total = acc[...]
        for d in range(4):
            rolled[d] = total if d == 0 else pltpu.roll(total, 32 * d, 1)
        quarter = lax.broadcasted_iota(jnp.int32, (4, LANES), 1) // 32
        for p in range(4):
            for j in range(TA):
                piece = jnp.zeros((4, LANES), f32)
                for g in range(4):
                    rows = rolled[(g - p) % 4, 16 * j + 4 * g : 16 * j + 4 * g + 4, :]
                    piece = jnp.where(quarter == g, rows, piece)
                out_ref[p * TA + j] = piece


def correlate(order, slabs, tail, toep, usum):
    c_loc = tail.shape[0]
    slab_spec = pl.BlockSpec((CB, SLAB), lambda i, o: (i, 0))
    return pl.pallas_call(
        correlate_kernel,
        grid_spec=pltpu.PrefetchScalarGridSpec(
            num_scalar_prefetch=1,
            grid=(c_loc // CB,),
            in_specs=[slab_spec] * (TA + 1)
            + [
                pl.BlockSpec((CB, K_LOC * B, 256), lambda i, o: (i, 0, 0)),
                pl.BlockSpec((K_LOC, c_loc), lambda i, o: (0, 0)),
            ],
            out_specs=pl.BlockSpec((32, 4, LANES), lambda i, o: (0, 0, 0)),
            scratch_shapes=[
                pltpu.VMEM((CB // 8, 8, (TA + 1) * SLAB), jnp.float32),
                pltpu.VMEM((CB, (TA + 1) * SLAB), jnp.bfloat16),
                pltpu.VMEM((CB // 8, 8, TA * SLAB), jnp.float32),
                pltpu.VMEM((c_loc, TA * SLAB), jnp.bfloat16),
                pltpu.VMEM((512, 256), jnp.bfloat16),
                pltpu.VMEM((LANES, LANES), jnp.float32),
                pltpu.VMEM((K_LOC, TA * SLAB), jnp.float32),
                pltpu.VMEM((4, LANES, LANES), jnp.float32),
            ],
        ),
        out_shape=jax.ShapeDtypeStruct((32, 4, LANES), jnp.float32),
        cost_estimate=pl.CostEstimate(flops=4 * 10**9, bytes_accessed=20 * 10**6, transcendentals=0),
        name="correlate",
    )(order, *slabs, tail, toep, usum)


def along_x(by):
    return [(i, i // 4 * 4 + (i + by) % 4) for i in range(TA)]


ACROSS_Z = [(i, (i + 4) % TA) for i in range(TA)]
TO_OWNER = [
    ((p * TA + j) * TA + a, (4 * a + p) * TA + j) for p in range(4) for j in range(TA) for a in range(TA)
]


def on_device(templates, record, record_tail):
    centre = jnp.mean(record_tail, axis=1, keepdims=True)
    own = (record - centre).astype(jnp.bfloat16)
    tail = (record_tail - centre).astype(jnp.bfloat16)
    tail = jnp.pad(tail, ((0, 0), (0, SLAB - tail.shape[1])))
    other = lax.ppermute(own, "ta", ACROSS_Z)
    slabs = [own, other]
    ta = lax.axis_index("ta")
    zh, x = ta // 4, ta % 4
    order = [ta, (1 - zh) * 4 + x]
    for by in (1, 2, 3):
        slabs.append(lax.ppermute(own, "ta", along_x(by)))
        order.append(zh * 4 + (x - by) % 4)
    for by in (1, 2, 3):
        slabs.append(lax.ppermute(other, "ta", along_x(by)))
        order.append((1 - zh) * 4 + (x - by) % 4)
    toep, usum = toeplitz(templates)
    part = correlate(jnp.stack(order).astype(jnp.int32), slabs, tail, toep, usum)
    summed = jnp.sum(lax.all_to_all(part, "ch", 0, 0), axis=0)
    mine = lax.ppermute(summed, ("ch", "ta"), TO_OWNER)
    mine = jnp.transpose(mine.reshape(4, 4, 2, B), (2, 1, 0, 3)).reshape(2, 2, 8, B)
    return jnp.flip(mine, 2).reshape(2, SLAB) * (1.0 / C)


def solution(mesh):
    return jax.shard_map(
        on_device,
        mesh=mesh,
        in_specs=(P("ta", None, "ch"), P("ch", "ta"), P("ch", None)),
        out_specs=P("ch", "ta"),
        check_vma=False,
    )
```

```python
import functools
import math

import jax
import jax.numpy as jnp
from jax import lax
from jax.experimental import pallas as pl
from jax.experimental.pallas import tpu as pltpu
from jax.sharding import PartitionSpec as P

C = 8192
M = 200
K_LOC = 8
B = 16
CB = 32
SLAB = 256
TA = 8
LANES = 128
TILES = 16


def toeplitz_kernel(t_ref, out_ref, sum_ref, ut, shift):
    half, sub = pl.program_id(0), pl.program_id(1)
    f32, bf16 = jnp.float32, jnp.bfloat16

    @pl.when((half == 0) & (sub == 0))
    def _():
        ahead = lax.broadcasted_iota(jnp.int32, (256, 256), 1) - lax.broadcasted_iota(
            jnp.int32, (256, 256), 0
        )
        for t0 in range(B // 2):
            shift[t0] = jnp.where(ahead == t0, 1.0, 0.0).astype(bf16)

    @pl.when(sub == 0)
    def _():
        for k in range(K_LOC):
            v = t_ref[k].astype(f32)
            v = v - jnp.sum(v, axis=0, keepdims=True) / M
            var = jnp.sum(v * v, axis=0, keepdims=True) / M
            unit = (v * lax.rsqrt(var + 1e-6) / math.sqrt(M)).astype(bf16).astype(f32)
            sum_ref[k : k + 1, :] = jnp.sum(unit, axis=0, keepdims=True)
            padded = jnp.concatenate([unit, jnp.zeros((256 - M, LANES), f32)], axis=0)
            turned = padded.T
            for i in range(2):
                ut[i, pl.ds(k, LANES, stride=K_LOC), :] = turned[:, LANES * i : LANES * i + LANES]

    here = pl.ds(pl.multiple_of(sub * (CB * K_LOC), CB * K_LOC), CB * K_LOC)
    rows = jnp.concatenate([ut[i, here, :] for i in range(2)], axis=1).astype(bf16)
    for pair in range(B // 4):
        moved = [
            jnp.dot(rows, shift[2 * pair + i], preferred_element_type=f32).reshape(CB, K_LOC, 256)
            for i in range(2)
        ]
        both = jnp.concatenate(moved, axis=1).astype(bf16)
        out_ref[:, 16 * pair : 16 * pair + 16, :] = both
        both = pltpu.roll(both.reshape(CB * 16, 256), B // 2, 1).reshape(CB, 16, 256)
        out_ref[:, 64 + 16 * pair : 80 + 16 * pair, :] = both


def toeplitz(templates):
    c_loc = templates.shape[2]
    return pl.pallas_call(
        toeplitz_kernel,
        grid=(c_loc // LANES, LANES // CB),
        in_specs=[pl.BlockSpec((K_LOC, M, LANES), lambda h, s: (0, 0, h))],
        out_specs=[
            pl.BlockSpec((CB, B * K_LOC, 256), lambda h, s: (h * (LANES // CB) + s, 0, 0)),
            pl.BlockSpec((K_LOC, LANES), lambda h, s: (0, h)),
        ],
        out_shape=[
            jax.ShapeDtypeStruct((c_loc, B * K_LOC, 256), jnp.bfloat16),
            jax.ShapeDtypeStruct((K_LOC, c_loc), jnp.float32),
        ],
        scratch_shapes=[
            pltpu.VMEM((2, LANES * K_LOC, LANES), jnp.float32),
            pltpu.VMEM((B // 2, 256, 256), jnp.bfloat16),
        ],
        cost_estimate=pl.CostEstimate(flops=10**9, bytes_accessed=18 * 10**6, transcendentals=0),
        name="toeplitz",
    )(templates)


def lag_of(n):
    return B * ((n % B) ^ 7) + n // B


def swap_chunks(tiles, lane):
    for d in (4, 2, 1):
        upper = (lane // B) % (2 * d) >= d
        swapped = []
        for b in range(TA):
            other = tiles[b ^ d]
            if b & d:
                swapped.append(jnp.where(upper, tiles[b], pltpu.roll(other, LANES - B * d, 1)))
            else:
                swapped.append(jnp.where(upper, pltpu.roll(other, B * d, 1), tiles[b]))
        tiles = swapped
    return tiles


def correlate_kernel(order, *refs):
    slabs = refs[:TA]
    tail_ref, toep_ref, usum_ref, out_ref = refs[TA : TA + 4]
    xa, xb, high, low, s_scr, mu_s, band, acc = refs[TA + 4 :]
    step = pl.program_id(0)
    f32, bf16 = jnp.float32, jnp.bfloat16
    groups = CB // 8

    @pl.when(step == 0)
    def _():
        j = lax.broadcasted_iota(jnp.int32, (512, 256), 0)
        n = lax.broadcasted_iota(jnp.int32, (512, 256), 1)
        t = lag_of(n)
        once = jnp.where((j >= t) & (j < t + M), 1.0, 0.0).astype(bf16)
        band[:512] = once
        band[512:] = once
        acc[...] = jnp.zeros_like(acc)

    def place(where, part):
        wide = part.astype(f32)
        square = wide * wide
        top = square.astype(bf16)
        xb[:, where] = part
        high[:, where] = top
        low[:, where] = (square - top.astype(f32)).astype(bf16)
        xa[:, :, where] = wide.reshape(groups, 8, SLAB)

    for i in range(TA):
        place(pl.ds(pl.multiple_of(order[i] * SLAB, SLAB), SLAB), slabs[i][...])
    place(pl.ds(TA * SLAB, SLAB), tail_ref[...])

    dot = functools.partial(jnp.dot, preferred_element_type=f32)
    spans = [slice(SLAB * b, SLAB * b + 512) for b in range(TA)]
    s1 = dot(jnp.concatenate([xb[:, span] for span in spans], axis=0), band[:512])
    s2 = dot(
        jnp.concatenate(
            [jnp.concatenate([high[:, span], low[:, span]], axis=1) for span in spans], axis=0
        ),
        band[...],
    )
    scale = lax.rsqrt(jnp.maximum(s2 - s1 * s1 * (1.0 / M), 0.0) + M * 1e-6)
    smu = (s1 * scale).astype(bf16)
    channels = pl.ds(pl.multiple_of(step * CB, CB), CB)
    for b in range(TA):
        mu_s[channels, SLAB * b : SLAB * b + SLAB] = smu[CB * b : CB * b + CB]
    lane = lax.broadcasted_iota(jnp.int32, (8, LANES), 1)
    for g in range(groups):
        for h in range(2):
            tiles = [
                scale[CB * b + 8 * g : CB * b + 8 * g + 8, LANES * h : LANES * h + LANES]
                for b in range(TA)
            ]
            for i, tile in enumerate(swap_chunks(tiles, lane)):
                s_scr[g, 8 * h + i] = tile

    back = 7 - lax.broadcasted_iota(jnp.int32, (8, LANES), 0)
    inside = lane + B * back < LANES
    total = [acc[8 * i : 8 * i + 8, :] for i in range(B)]
    for g in range(groups):
        for cc in range(8):
            turned = []
            for q in range(TILES + 2):
                row = xa[g, cc : cc + 1, LANES * q : LANES * q + LANES]
                row = jnp.broadcast_to(row, (8, LANES))
                turned.append(pltpu.roll(row, B, 1, stride=B, stride_axis=0))
            tiles = [jnp.where(inside, turned[q], turned[q + 1]) for q in range(TILES + 1)]
            x0 = jnp.concatenate(tiles[:TILES], axis=0).astype(bf16)
            x1 = jnp.concatenate(tiles[1:], axis=0).astype(bf16)
            x = jnp.concatenate([x0, x1], axis=1)
            prod = lax.dot_general(
                toep_ref[g * 8 + cc], x, (((1,), (1,)), ((), ())), preferred_element_type=f32
            )
            for i in range(B):
                factor = jnp.broadcast_to(s_scr[g, i, cc : cc + 1, :], (8, LANES))
                total[i] = total[i] + prod[8 * i : 8 * i + 8, :] * factor
    for i in range(B):
        acc[8 * i : 8 * i + 8, :] = total[i]

    @pl.when(step == pl.num_programs(0) - 1)
    def _():
        usum = usum_ref[...] * (1.0 / M)
        uh = usum.astype(bf16)
        ul = (usum - uh.astype(f32)).astype(bf16)
        smu = mu_s[...]
        fix = dot(uh, smu) + dot(ul, smu)
        halves = []
        for h in range(2):
            cols = [SLAB * b + LANES * h for b in range(TA)]
            fixes = swap_chunks([fix[:, c : c + LANES] for c in cols], lane)
            rows = [acc[64 * h + 8 * i : 64 * h + 8 * i + 8, :] - fixes[i] for i in range(TA)]
            halves.append(jnp.concatenate(swap_chunks(rows, lane), axis=0))
        value = jnp.concatenate(halves, axis=1) * (1.0 / C)
        n = lax.broadcasted_iota(jnp.int32, (SLAB, SLAB), 0)
        t = lax.broadcasted_iota(jnp.int32, (SLAB, SLAB), 1)
        to_lag = jnp.where(t == lag_of(n), 1.0, 0.0).astype(bf16)
        v1 = value.astype(bf16)
        rest = value - v1.astype(f32)
        v2 = rest.astype(bf16)
        v3 = (rest - v2.astype(f32)).astype(bf16)
        value = dot(v1, to_lag) + dot(v2, to_lag) + dot(v3, to_lag)
        for i in range(32):
            out_ref[i] = value[2 * i : 2 * i + 2, :]


def correlate(order, slabs, tail, toep, usum):
    c_loc = tail.shape[0]
    slab_spec = pl.BlockSpec((CB, SLAB), lambda i, o: (i, 0))
    return pl.pallas_call(
        correlate_kernel,
        grid_spec=pltpu.PrefetchScalarGridSpec(
            num_scalar_prefetch=1,
            grid=(c_loc // CB,),
            in_specs=[slab_spec] * (TA + 1)
            + [
                pl.BlockSpec((CB, K_LOC * B, 256), lambda i, o: (i, 0, 0)),
                pl.BlockSpec((K_LOC, c_loc), lambda i, o: (0, 0)),
            ],
            out_specs=pl.BlockSpec((32, 2, SLAB), lambda i, o: (0, 0, 0)),
            scratch_shapes=[
                pltpu.VMEM((CB // 8, 8, (TA + 1) * SLAB), jnp.float32),
                pltpu.VMEM((CB, (TA + 1) * SLAB), jnp.bfloat16),
                pltpu.VMEM((CB, (TA + 1) * SLAB), jnp.bfloat16),
                pltpu.VMEM((CB, (TA + 1) * SLAB), jnp.bfloat16),
                pltpu.VMEM((CB // 8, B, 8, LANES), jnp.float32),
                pltpu.VMEM((c_loc, TA * SLAB), jnp.bfloat16),
                pltpu.VMEM((1024, 256), jnp.bfloat16),
                pltpu.VMEM((LANES, LANES), jnp.float32),
            ],
        ),
        out_shape=jax.ShapeDtypeStruct((32, 2, SLAB), jnp.float32),
        cost_estimate=pl.CostEstimate(flops=4 * 10**9, bytes_accessed=20 * 10**6, transcendentals=0),
        name="correlate",
    )(order, *slabs, tail, toep, usum)


def along_x(by):
    return [(i, i // 4 * 4 + (i + by) % 4) for i in range(TA)]


ACROSS_Z = [(i, (i + 4) % TA) for i in range(TA)]
TO_OWNER = [
    ((4 * j + p) * TA + a, (4 * a + p) * TA + j) for j in range(TA) for p in range(4) for a in range(TA)
]


def on_device(templates, record, record_tail):
    centre = jnp.mean(record_tail, axis=1, keepdims=True)
    own = (record - centre).astype(jnp.bfloat16)
    tail = (record_tail - centre).astype(jnp.bfloat16)
    tail = jnp.pad(tail, ((0, 0), (0, SLAB - tail.shape[1])))
    other = lax.ppermute(own, "ta", ACROSS_Z)
    slabs = [own, other]
    ta = lax.axis_index("ta")
    zh, x = ta // 4, ta % 4
    order = [ta, (1 - zh) * 4 + x]
    for by in (1, 2, 3):
        slabs.append(lax.ppermute(own, "ta", along_x(by)))
        order.append(zh * 4 + (x - by) % 4)
    for by in (1, 2, 3):
        slabs.append(lax.ppermute(other, "ta", along_x(by)))
        order.append((1 - zh) * 4 + (x - by) % 4)
    toep, usum = toeplitz(templates)
    part = correlate(jnp.stack(order).astype(jnp.int32), slabs, tail, toep, usum)
    summed = jnp.sum(lax.all_to_all(part, "ch", 0, 0), axis=0)
    return lax.ppermute(summed, ("ch", "ta"), TO_OWNER)


def solution(mesh):
    return jax.shard_map(
        on_device,
        mesh=mesh,
        in_specs=(P("ta", None, "ch"), P("ch", "ta"), P("ch", None)),
        out_specs=P("ch", "ta"),
        check_vma=False,
    )
```

```python
import functools
import math

import jax
import jax.numpy as jnp
from jax import lax
from jax.experimental import pallas as pl
from jax.experimental.pallas import tpu as pltpu
from jax.sharding import PartitionSpec as P

C = 8192
M = 200
K_LOC = 8
B = 16
CB = 32
SLAB = 256
TA = 8
LANES = 128
TILES = 16


def centre_kernel(record_ref, tail_ref, own_ref, tail_out):
    tail = tail_ref[...]
    centre = jnp.sum(tail, axis=0, keepdims=True) / tail.shape[0]
    fill = jnp.zeros((SLAB - tail.shape[0], tail.shape[1]), jnp.float32)
    tail_out[...] = jnp.concatenate([tail - centre, fill], axis=0).T.astype(jnp.bfloat16)
    column = jnp.broadcast_to(centre, (LANES, centre.shape[1])).T
    for i in range(SLAB // LANES):
        span = slice(LANES * i, LANES * i + LANES)
        own_ref[:, span] = (record_ref[:, span] - column).astype(jnp.bfloat16)


def centred(record, record_tail):
    shape = jax.ShapeDtypeStruct(record.shape, jnp.bfloat16)
    return pl.pallas_call(centre_kernel, out_shape=[shape, shape], name="centre")(
        record, jnp.transpose(record_tail)
    )


def unit_kernel(t_ref, out_ref, sum_ref, ut):
    f32, bf16 = jnp.float32, jnp.bfloat16
    for k in range(K_LOC):
        v = t_ref[k].astype(f32)
        v = v - jnp.sum(v, axis=0, keepdims=True) / M
        var = jnp.sum(v * v, axis=0, keepdims=True) / M
        unit = (v * lax.rsqrt(var + 1e-6) / math.sqrt(M)).astype(bf16).astype(f32)
        sum_ref[k : k + 1, :] = jnp.sum(unit, axis=0, keepdims=True)
        padded = jnp.concatenate([unit, jnp.zeros((256 - M, LANES), f32)], axis=0)
        turned = padded.T
        for i in range(2):
            ut[i, pl.ds(k, LANES, stride=K_LOC), :] = turned[:, LANES * i : LANES * i + LANES]
    out_ref[...] = jnp.concatenate([ut[i] for i in range(2)], axis=1).astype(bf16)


def units(templates):
    c_loc = templates.shape[2]
    return pl.pallas_call(
        unit_kernel,
        grid=(c_loc // LANES,),
        in_specs=[pl.BlockSpec((K_LOC, M, LANES), lambda h: (0, 0, h))],
        out_specs=[
            pl.BlockSpec((LANES * K_LOC, 256), lambda h: (h, 0)),
            pl.BlockSpec((K_LOC, LANES), lambda h: (0, h)),
        ],
        out_shape=[
            jax.ShapeDtypeStruct((c_loc * K_LOC, 256), jnp.bfloat16),
            jax.ShapeDtypeStruct((K_LOC, c_loc), jnp.float32),
        ],
        scratch_shapes=[pltpu.VMEM((2, LANES * K_LOC, LANES), jnp.float32)],
        cost_estimate=pl.CostEstimate(flops=10**8, bytes_accessed=9 * 10**6, transcendentals=0),
        name="units",
    )(templates)


def lag_of(n):
    return B * ((n % B) ^ 7) + n // B


def swap_chunks(tiles, lane):
    for d in (4, 2, 1):
        upper = (lane // B) % (2 * d) >= d
        swapped = []
        for b in range(TA):
            other = tiles[b ^ d]
            if b & d:
                swapped.append(jnp.where(upper, tiles[b], pltpu.roll(other, LANES - B * d, 1)))
            else:
                swapped.append(jnp.where(upper, pltpu.roll(other, B * d, 1), tiles[b]))
        tiles = swapped
    return tiles


def correlate_kernel(place_ref, *refs):
    slabs = refs[:TA]
    tail_ref, unit_ref, usum_ref, out_ref = refs[TA : TA + 4]
    xa, xb, high, low, s_scr, mu_s, band, shift, toep, acc = refs[TA + 4 :]
    step = pl.program_id(0)
    f32, bf16 = jnp.float32, jnp.bfloat16
    groups = CB // 8

    @pl.when(step == 0)
    def _():
        j = lax.broadcasted_iota(jnp.int32, (512, 256), 0)
        n = lax.broadcasted_iota(jnp.int32, (512, 256), 1)
        t = lag_of(n)
        once = jnp.where((j >= t) & (j < t + M), 1.0, 0.0).astype(bf16)
        band[:512] = once
        band[512:] = once
        acc[...] = jnp.zeros_like(acc)
        ahead = lax.broadcasted_iota(jnp.int32, (256, 256), 1) - lax.broadcasted_iota(
            jnp.int32, (256, 256), 0
        )
        for t0 in range(B // 2):
            shift[t0] = jnp.where(ahead == t0, 1.0, 0.0).astype(bf16)

    rows = unit_ref[...]
    for pair in range(B // 4):
        moved = [
            jnp.dot(rows, shift[2 * pair + i], preferred_element_type=f32).reshape(CB, K_LOC, 256)
            for i in range(2)
        ]
        both = jnp.concatenate(moved, axis=1).astype(bf16)
        toep[:, 16 * pair : 16 * pair + 16, :] = both
        both = pltpu.roll(both.reshape(CB * 16, 256), B // 2, 1).reshape(CB, 16, 256)
        toep[:, 64 + 16 * pair : 80 + 16 * pair, :] = both

    def place(where, part):
        wide = part.astype(f32)
        square = wide * wide
        top = square.astype(bf16)
        xb[:, where] = part
        high[:, where] = top
        low[:, where] = (square - top.astype(f32)).astype(bf16)
        xa[:, :, where] = wide.reshape(groups, 8, SLAB)

    half, x = place_ref[0] // 4, place_ref[0] % 4
    for i in range(TA):
        slab = (half if i < 4 else 1 - half) * 4 + (x + 4 - i % 4) % 4
        place(pl.ds(pl.multiple_of(slab * SLAB, SLAB), SLAB), slabs[i][...])
    place(pl.ds(TA * SLAB, SLAB), tail_ref[...])

    dot = functools.partial(jnp.dot, preferred_element_type=f32)
    spans = [slice(SLAB * b, SLAB * b + 512) for b in range(TA)]
    s1 = dot(jnp.concatenate([xb[:, span] for span in spans], axis=0), band[:512])
    s2 = dot(
        jnp.concatenate(
            [jnp.concatenate([high[:, span], low[:, span]], axis=1) for span in spans], axis=0
        ),
        band[...],
    )
    scale = lax.rsqrt(jnp.maximum(s2 - s1 * s1 * (1.0 / M), 0.0) + M * 1e-6)
    smu = (s1 * scale).astype(bf16)
    channels = pl.ds(pl.multiple_of(step * CB, CB), CB)
    for b in range(TA):
        mu_s[channels, SLAB * b : SLAB * b + SLAB] = smu[CB * b : CB * b + CB]
    lane = lax.broadcasted_iota(jnp.int32, (8, LANES), 1)
    for g in range(groups):
        for h in range(2):
            tiles = [
                scale[CB * b + 8 * g : CB * b + 8 * g + 8, LANES * h : LANES * h + LANES]
                for b in range(TA)
            ]
            for i, tile in enumerate(swap_chunks(tiles, lane)):
                s_scr[g, 8 * h + i] = tile

    back = 7 - lax.broadcasted_iota(jnp.int32, (8, LANES), 0)
    inside = lane + B * back < LANES
    total = [acc[8 * i : 8 * i + 8, :] for i in range(B)]
    for g in range(groups):
        for cc in range(8):
            turned = []
            for q in range(TILES + 2):
                row = xa[g, cc : cc + 1, LANES * q : LANES * q + LANES]
                row = jnp.broadcast_to(row, (8, LANES))
                turned.append(pltpu.roll(row, B, 1, stride=B, stride_axis=0))
            tiles = [jnp.where(inside, turned[q], turned[q + 1]) for q in range(TILES + 1)]
            x0 = jnp.concatenate(tiles[:TILES], axis=0).astype(bf16)
            x1 = jnp.concatenate(tiles[1:], axis=0).astype(bf16)
            x = jnp.concatenate([x0, x1], axis=1)
            prod = lax.dot_general(
                toep[g * 8 + cc], x, (((1,), (1,)), ((), ())), preferred_element_type=f32
            )
            for i in range(B):
                factor = jnp.broadcast_to(s_scr[g, i, cc : cc + 1, :], (8, LANES))
                total[i] = total[i] + prod[8 * i : 8 * i + 8, :] * factor
    for i in range(B):
        acc[8 * i : 8 * i + 8, :] = total[i]

    @pl.when(step == pl.num_programs(0) - 1)
    def _():
        usum = usum_ref[...] * (1.0 / M)
        uh = usum.astype(bf16)
        ul = (usum - uh.astype(f32)).astype(bf16)
        smu = mu_s[...]
        fix = dot(uh, smu) + dot(ul, smu)
        halves = []
        for h in range(2):
            cols = [SLAB * b + LANES * h for b in range(TA)]
            fixes = swap_chunks([fix[:, c : c + LANES] for c in cols], lane)
            rows = [acc[64 * h + 8 * i : 64 * h + 8 * i + 8, :] - fixes[i] for i in range(TA)]
            halves.append(jnp.concatenate(swap_chunks(rows, lane), axis=0))
        value = jnp.concatenate(halves, axis=1) * (1.0 / C)
        n = lax.broadcasted_iota(jnp.int32, (SLAB, SLAB), 0)
        t = lax.broadcasted_iota(jnp.int32, (SLAB, SLAB), 1)
        to_lag = jnp.where(t == lag_of(n), 1.0, 0.0).astype(bf16)
        v1 = value.astype(bf16)
        rest = value - v1.astype(f32)
        v2 = rest.astype(bf16)
        v3 = (rest - v2.astype(f32)).astype(bf16)
        value = dot(v1, to_lag) + dot(v2, to_lag) + dot(v3, to_lag)
        for i in range(32):
            out_ref[i] = value[2 * i : 2 * i + 2, :]


def correlate(place, slabs, tail, unit, usum):
    c_loc = tail.shape[0]
    slab_spec = pl.BlockSpec((CB, SLAB), lambda i, o: (i, 0))
    return pl.pallas_call(
        correlate_kernel,
        grid_spec=pltpu.PrefetchScalarGridSpec(
            num_scalar_prefetch=1,
            grid=(c_loc // CB,),
            in_specs=[slab_spec] * (TA + 1)
            + [
                pl.BlockSpec((CB * K_LOC, 256), lambda i, o: (i, 0)),
                pl.BlockSpec((K_LOC, c_loc), lambda i, o: (0, 0)),
            ],
            out_specs=pl.BlockSpec((32, 2, SLAB), lambda i, o: (0, 0, 0)),
            scratch_shapes=[
                pltpu.VMEM((CB // 8, 8, (TA + 1) * SLAB), jnp.float32),
                pltpu.VMEM((CB, (TA + 1) * SLAB), jnp.bfloat16),
                pltpu.VMEM((CB, (TA + 1) * SLAB), jnp.bfloat16),
                pltpu.VMEM((CB, (TA + 1) * SLAB), jnp.bfloat16),
                pltpu.VMEM((CB // 8, B, 8, LANES), jnp.float32),
                pltpu.VMEM((c_loc, TA * SLAB), jnp.bfloat16),
                pltpu.VMEM((1024, 256), jnp.bfloat16),
                pltpu.VMEM((B // 2, 256, 256), jnp.bfloat16),
                pltpu.VMEM((CB, K_LOC * B, 256), jnp.bfloat16),
                pltpu.VMEM((LANES, LANES), jnp.float32),
            ],
        ),
        out_shape=jax.ShapeDtypeStruct((32, 2, SLAB), jnp.float32),
        cost_estimate=pl.CostEstimate(flops=4 * 10**9, bytes_accessed=20 * 10**6, transcendentals=0),
        name="correlate",
    )(place, *slabs, tail, unit, usum)


def along_x(by):
    return [(i, i // 4 * 4 + (i + by) % 4) for i in range(TA)]


ACROSS_Z = [(i, (i + 4) % TA) for i in range(TA)]
TO_OWNER = [
    ((4 * j + p) * TA + a, (4 * a + p) * TA + j) for j in range(TA) for p in range(4) for a in range(TA)
]


def on_device(templates, record, record_tail):
    own, tail = centred(record, record_tail)
    other = lax.ppermute(own, "ta", ACROSS_Z)
    slabs = [own] + [lax.ppermute(own, "ta", along_x(by)) for by in (1, 2, 3)]
    slabs += [other] + [lax.ppermute(other, "ta", along_x(by)) for by in (1, 2, 3)]
    place = lax.axis_index("ta").astype(jnp.int32).reshape(1)
    unit, usum = units(templates)
    part = correlate(place, slabs, tail, unit, usum)
    summed = jnp.sum(lax.all_to_all(part, "ch", 0, 0), axis=0)
    return lax.ppermute(summed, ("ch", "ta"), TO_OWNER)


def solution(mesh):
    return jax.shard_map(
        on_device,
        mesh=mesh,
        in_specs=(P("ta", None, "ch"), P("ch", "ta"), P("ch", None)),
        out_specs=P("ch", "ta"),
        check_vma=False,
    )
```

```python
import functools
import math

import jax
import jax.numpy as jnp
from jax import lax
from jax.experimental import pallas as pl
from jax.experimental.pallas import tpu as pltpu
from jax.sharding import PartitionSpec as P

C = 8192
M = 200
K_LOC = 8
B = 16
CB = 64
SLAB = 256
TA = 8
LANES = 128
TILES = 16


def centre_of(tail):
    return jnp.sum(tail, axis=0, keepdims=True) / tail.shape[0]


def centre_kernel(record_ref, tail_ref, own_ref):
    centre = centre_of(tail_ref[...])
    column = jnp.broadcast_to(centre, (LANES, centre.shape[1])).T
    for i in range(SLAB // LANES):
        span = slice(LANES * i, LANES * i + LANES)
        own_ref[:, span] = (record_ref[:, span] - column).astype(jnp.bfloat16)


def centred(record, late):
    shape = jax.ShapeDtypeStruct(record.shape, jnp.bfloat16)
    return pl.pallas_call(
        centre_kernel,
        out_shape=shape,
        compiler_params=pltpu.CompilerParams(vmem_limit_bytes=8 << 20),
        name="centre",
    )(record, late)


def unit_kernel(t_ref, late_ref, out_ref, sum_ref, tail_ref, ut):
    f32, bf16 = jnp.float32, jnp.bfloat16
    late = late_ref[...]
    fill = jnp.zeros((SLAB - late.shape[0], late.shape[1]), f32)
    tail_ref[...] = jnp.concatenate([late - centre_of(late), fill], axis=0).T.astype(bf16)
    for k in range(K_LOC):
        v = t_ref[k].astype(f32)
        v = v - jnp.sum(v, axis=0, keepdims=True) / M
        var = jnp.sum(v * v, axis=0, keepdims=True) / M
        unit = (v * lax.rsqrt(var + 1e-6) / math.sqrt(M)).astype(bf16).astype(f32)
        sum_ref[k : k + 1, :] = jnp.sum(unit, axis=0, keepdims=True)
        padded = jnp.concatenate([unit, jnp.zeros((256 - M, LANES), f32)], axis=0)
        turned = padded.T
        for i in range(2):
            ut[i, pl.ds(k, LANES, stride=K_LOC), :] = turned[:, LANES * i : LANES * i + LANES]
    out_ref[...] = jnp.concatenate([ut[i] for i in range(2)], axis=1).astype(bf16)


def units(templates, late):
    c_loc = templates.shape[2]
    return pl.pallas_call(
        unit_kernel,
        grid=(c_loc // LANES,),
        in_specs=[
            pl.BlockSpec((K_LOC, M, LANES), lambda h: (0, 0, h)),
            pl.BlockSpec((late.shape[0], LANES), lambda h: (0, h)),
        ],
        out_specs=[
            pl.BlockSpec((LANES * K_LOC, 256), lambda h: (h, 0)),
            pl.BlockSpec((K_LOC, LANES), lambda h: (0, h)),
            pl.BlockSpec((LANES, SLAB), lambda h: (h, 0)),
        ],
        out_shape=[
            jax.ShapeDtypeStruct((c_loc * K_LOC, 256), jnp.bfloat16),
            jax.ShapeDtypeStruct((K_LOC, c_loc), jnp.float32),
            jax.ShapeDtypeStruct((c_loc, SLAB), jnp.bfloat16),
        ],
        scratch_shapes=[pltpu.VMEM((2, LANES * K_LOC, LANES), jnp.float32)],
        compiler_params=pltpu.CompilerParams(vmem_limit_bytes=20 << 20),
        cost_estimate=pl.CostEstimate(flops=10**8, bytes_accessed=9 * 10**6, transcendentals=0),
        name="units",
    )(templates, late)


def lag_of(n):
    return B * ((n % B) ^ 7) + n // B


def swap_chunks(tiles, lane):
    for d in (4, 2, 1):
        upper = (lane // B) % (2 * d) >= d
        swapped = []
        for b in range(TA):
            other = tiles[b ^ d]
            if b & d:
                swapped.append(jnp.where(upper, tiles[b], pltpu.roll(other, LANES - B * d, 1)))
            else:
                swapped.append(jnp.where(upper, pltpu.roll(other, B * d, 1), tiles[b]))
        tiles = swapped
    return tiles


def correlate_kernel(place_ref, *refs):
    slabs = refs[:TA]
    tail_ref, unit_ref, usum_ref, out_ref = refs[TA : TA + 4]
    xa, xb, high, low, s_scr, mu_s, band, shift, toep, acc = refs[TA + 4 :]
    step = pl.program_id(0)
    f32, bf16 = jnp.float32, jnp.bfloat16
    groups = CB // 8

    @pl.when(step == 0)
    def _():
        j = lax.broadcasted_iota(jnp.int32, (512, 256), 0)
        n = lax.broadcasted_iota(jnp.int32, (512, 256), 1)
        t = lag_of(n)
        once = jnp.where((j >= t) & (j < t + M), 1.0, 0.0).astype(bf16)
        band[:512] = once
        band[512:] = once
        acc[...] = jnp.zeros_like(acc)
        ahead = lax.broadcasted_iota(jnp.int32, (256, 256), 1) - lax.broadcasted_iota(
            jnp.int32, (256, 256), 0
        )
        for t0 in range(B // 2):
            shift[t0] = jnp.where(ahead == t0, 1.0, 0.0).astype(bf16)

    rows = unit_ref[...]
    for pair in range(B // 4):
        moved = [
            jnp.dot(rows, shift[2 * pair + i], preferred_element_type=f32).reshape(CB, K_LOC, 256)
            for i in range(2)
        ]
        both = jnp.concatenate(moved, axis=1).astype(bf16)
        toep[:, 16 * pair : 16 * pair + 16, :] = both
        both = pltpu.roll(both.reshape(CB * 16, 256), B // 2, 1).reshape(CB, 16, 256)
        toep[:, 64 + 16 * pair : 80 + 16 * pair, :] = both

    def place(where, part):
        wide = part.astype(f32)
        square = wide * wide
        top = square.astype(bf16)
        xb[:, where] = part
        high[:, where] = top
        low[:, where] = (square - top.astype(f32)).astype(bf16)
        xa[:, :, where] = wide.reshape(groups, 8, SLAB)

    half, x = place_ref[0] // 4, place_ref[0] % 4
    for i in range(TA):
        slab = (half if i < 4 else 1 - half) * 4 + (x + 4 - i % 4) % 4
        place(pl.ds(pl.multiple_of(slab * SLAB, SLAB), SLAB), slabs[i][...])
    place(pl.ds(TA * SLAB, SLAB), tail_ref[...])

    dot = functools.partial(jnp.dot, preferred_element_type=f32)
    spans = [slice(SLAB * b, SLAB * b + 512) for b in range(TA)]
    s1 = dot(jnp.concatenate([xb[:, span] for span in spans], axis=0), band[:512])
    s2 = dot(
        jnp.concatenate(
            [jnp.concatenate([high[:, span], low[:, span]], axis=1) for span in spans], axis=0
        ),
        band[...],
    )
    scale = lax.rsqrt(jnp.maximum(s2 - s1 * s1 * (1.0 / M), 0.0) + M * 1e-6)
    smu = (s1 * scale).astype(bf16)
    channels = pl.ds(pl.multiple_of(step * CB, CB), CB)
    for b in range(TA):
        mu_s[channels, SLAB * b : SLAB * b + SLAB] = smu[CB * b : CB * b + CB]
    lane = lax.broadcasted_iota(jnp.int32, (8, LANES), 1)
    for g in range(groups):
        for h in range(2):
            tiles = [
                scale[CB * b + 8 * g : CB * b + 8 * g + 8, LANES * h : LANES * h + LANES]
                for b in range(TA)
            ]
            for i, tile in enumerate(swap_chunks(tiles, lane)):
                s_scr[g, 8 * h + i] = tile

    back = 7 - lax.broadcasted_iota(jnp.int32, (8, LANES), 0)
    inside = lane + B * back < LANES
    total = [acc[8 * i : 8 * i + 8, :] for i in range(B)]
    for g in range(groups):
        for cc in range(8):
            turned = []
            for q in range(TILES + 2):
                row = xa[g, cc : cc + 1, LANES * q : LANES * q + LANES]
                row = jnp.broadcast_to(row, (8, LANES))
                turned.append(pltpu.roll(row, B, 1, stride=B, stride_axis=0))
            tiles = [jnp.where(inside, turned[q], turned[q + 1]) for q in range(TILES + 1)]
            x0 = jnp.concatenate(tiles[:TILES], axis=0).astype(bf16)
            x1 = jnp.concatenate(tiles[1:], axis=0).astype(bf16)
            x = jnp.concatenate([x0, x1], axis=1)
            prod = lax.dot_general(
                toep[g * 8 + cc], x, (((1,), (1,)), ((), ())), preferred_element_type=f32
            )
            for i in range(B):
                factor = jnp.broadcast_to(s_scr[g, i, cc : cc + 1, :], (8, LANES))
                total[i] = total[i] + prod[8 * i : 8 * i + 8, :] * factor
    for i in range(B):
        acc[8 * i : 8 * i + 8, :] = total[i]

    @pl.when(step == pl.num_programs(0) - 1)
    def _():
        usum = usum_ref[...] * (1.0 / M)
        uh = usum.astype(bf16)
        ul = (usum - uh.astype(f32)).astype(bf16)
        smu = mu_s[...]
        fix = dot(uh, smu) + dot(ul, smu)
        halves = []
        for h in range(2):
            cols = [SLAB * b + LANES * h for b in range(TA)]
            fixes = swap_chunks([fix[:, c : c + LANES] for c in cols], lane)
            rows = [acc[64 * h + 8 * i : 64 * h + 8 * i + 8, :] - fixes[i] for i in range(TA)]
            halves.append(jnp.concatenate(swap_chunks(rows, lane), axis=0))
        value = jnp.concatenate(halves, axis=1) * (1.0 / C)
        n = lax.broadcasted_iota(jnp.int32, (SLAB, SLAB), 0)
        t = lax.broadcasted_iota(jnp.int32, (SLAB, SLAB), 1)
        to_lag = jnp.where(t == lag_of(n), 1.0, 0.0).astype(bf16)
        v1 = value.astype(bf16)
        rest = value - v1.astype(f32)
        v2 = rest.astype(bf16)
        v3 = (rest - v2.astype(f32)).astype(bf16)
        value = dot(v1, to_lag) + dot(v2, to_lag) + dot(v3, to_lag)
        for i in range(32):
            out_ref[i] = value[2 * i : 2 * i + 2, :]


def correlate(place, slabs, tail, unit, usum):
    c_loc = tail.shape[0]
    slab_spec = pl.BlockSpec((CB, SLAB), lambda i, o: (i, 0))
    return pl.pallas_call(
        correlate_kernel,
        grid_spec=pltpu.PrefetchScalarGridSpec(
            num_scalar_prefetch=1,
            grid=(c_loc // CB,),
            in_specs=[slab_spec] * (TA + 1)
            + [
                pl.BlockSpec((CB * K_LOC, 256), lambda i, o: (i, 0)),
                pl.BlockSpec((K_LOC, c_loc), lambda i, o: (0, 0)),
            ],
            out_specs=pl.BlockSpec((32, 2, SLAB), lambda i, o: (0, 0, 0)),
            scratch_shapes=[
                pltpu.VMEM((CB // 8, 8, (TA + 1) * SLAB), jnp.float32),
                pltpu.VMEM((CB, (TA + 1) * SLAB), jnp.bfloat16),
                pltpu.VMEM((CB, (TA + 1) * SLAB), jnp.bfloat16),
                pltpu.VMEM((CB, (TA + 1) * SLAB), jnp.bfloat16),
                pltpu.VMEM((CB // 8, B, 8, LANES), jnp.float32),
                pltpu.VMEM((c_loc, TA * SLAB), jnp.bfloat16),
                pltpu.VMEM((1024, 256), jnp.bfloat16),
                pltpu.VMEM((B // 2, 256, 256), jnp.bfloat16),
                pltpu.VMEM((CB, K_LOC * B, 256), jnp.bfloat16),
                pltpu.VMEM((LANES, LANES), jnp.float32),
            ],
        ),
        out_shape=jax.ShapeDtypeStruct((32, 2, SLAB), jnp.float32),
        compiler_params=pltpu.CompilerParams(vmem_limit_bytes=24 << 20),
        cost_estimate=pl.CostEstimate(flops=4 * 10**9, bytes_accessed=20 * 10**6, transcendentals=0),
        name="correlate",
    )(place, *slabs, tail, unit, usum)


def along_x(by):
    return [(i, i // 4 * 4 + (i + by) % 4) for i in range(TA)]


ACROSS_Z = [(i, (i + 4) % TA) for i in range(TA)]
TO_OWNER = [
    ((4 * j + p) * TA + a, (4 * a + p) * TA + j) for j in range(TA) for p in range(4) for a in range(TA)
]


def on_device(templates, record, record_tail):
    late = jnp.transpose(record_tail)
    own = centred(record, late)
    other = lax.ppermute(own, "ta", ACROSS_Z)
    slabs = [own] + [lax.ppermute(own, "ta", along_x(by)) for by in (1, 2, 3)]
    slabs += [
        other,
        lax.ppermute(other, "ta", along_x(1)),
        lax.ppermute(slabs[2], "ta", ACROSS_Z),
        lax.ppermute(other, "ta", along_x(3)),
    ]
    place = lax.axis_index("ta").astype(jnp.int32).reshape(1)
    unit, usum, tail = units(templates, late)
    part = correlate(place, slabs, tail, unit, usum)
    summed = jnp.sum(lax.all_to_all(part, "ch", 0, 0), axis=0)
    return lax.ppermute(summed, ("ch", "ta"), TO_OWNER)


def solution(mesh):
    return jax.shard_map(
        on_device,
        mesh=mesh,
        in_specs=(P("ta", None, "ch"), P("ch", "ta"), P("ch", None)),
        out_specs=P("ch", "ta"),
        check_vma=False,
    )
```

```python
import functools
import math

import jax
import jax.numpy as jnp
from jax import lax
from jax.experimental import pallas as pl
from jax.experimental.pallas import tpu as pltpu
from jax.sharding import PartitionSpec as P

C = 8192
M = 200
K_LOC = 8
B = 16
CB = 64
TB = 64
SLAB = 256
TA = 8
LANES = 128
TILES = 16


def centre_of(tail):
    return jnp.sum(tail, axis=0, keepdims=True) / tail.shape[0]


def centre_kernel(record_hbm, late_hbm, own_ref, record, late, sems):
    copies = [
        pltpu.make_async_copy(late_hbm, late, sems.at[0]),
        pltpu.make_async_copy(record_hbm, record, sems.at[1]),
    ]
    for copy in copies:
        copy.start()
    copies[0].wait()
    centre = centre_of(late[...])
    column = jnp.broadcast_to(centre, (LANES, centre.shape[1])).T
    copies[1].wait()
    for i in range(SLAB // LANES):
        span = slice(LANES * i, LANES * i + LANES)
        own_ref[:, span] = (record[:, span] - column).astype(jnp.bfloat16)


def centred(record, late):
    return pl.pallas_call(
        centre_kernel,
        in_specs=[pl.BlockSpec(memory_space=pltpu.HBM)] * 2,
        out_specs=pl.BlockSpec(memory_space=pltpu.VMEM),
        out_shape=jax.ShapeDtypeStruct(record.shape, jnp.bfloat16),
        scratch_shapes=[
            pltpu.VMEM(record.shape, jnp.float32),
            pltpu.VMEM(late.shape, jnp.float32),
            pltpu.SemaphoreType.DMA((2,)),
        ],
        compiler_params=pltpu.CompilerParams(vmem_limit_bytes=8 << 20),
        name="centre",
    )(record, late)


def unit_kernel(t_ref, late_ref, toep, sum_ref, tail_ref, band, to_lag, ut, shift):
    f32, bf16 = jnp.float32, jnp.bfloat16
    late = late_ref[...]
    fill = jnp.zeros((SLAB - late.shape[0], late.shape[1]), f32)
    tail_ref[...] = jnp.concatenate([late - centre_of(late), fill], axis=0).T.astype(bf16)
    for k in range(K_LOC):
        v = t_ref[k].astype(f32)
        v = v - jnp.sum(v, axis=0, keepdims=True) / M
        var = jnp.sum(v * v, axis=0, keepdims=True) / M
        unit = (v * lax.rsqrt(var + 1e-6) / math.sqrt(M)).astype(bf16).astype(f32)
        sum_ref[k : k + 1, :] = jnp.sum(unit, axis=0, keepdims=True)
        padded = jnp.concatenate([unit, jnp.zeros((256 - M, LANES), f32)], axis=0)
        turned = padded.T
        for i in range(2):
            ut[i, pl.ds(k, LANES, stride=K_LOC), :] = turned[:, LANES * i : LANES * i + LANES]

    half = pl.program_id(0)

    @pl.when(half == 0)
    def _():
        ahead = lax.broadcasted_iota(jnp.int32, (256, 256), 1) - lax.broadcasted_iota(
            jnp.int32, (256, 256), 0
        )
        for t0 in range(B // 2):
            shift[t0] = jnp.where(ahead == t0, 1.0, 0.0).astype(bf16)
        j = lax.broadcasted_iota(jnp.int32, (512, 256), 0)
        t = lag_of(lax.broadcasted_iota(jnp.int32, (512, 256), 1))
        once = jnp.where((j >= t) & (j < t + M), 1.0, 0.0).astype(bf16)
        band[:512] = once
        band[512:] = once
        n = lax.broadcasted_iota(jnp.int32, (SLAB, SLAB), 0)
        t = lax.broadcasted_iota(jnp.int32, (SLAB, SLAB), 1)
        to_lag[...] = jnp.where(t == lag_of(n), 1.0, 0.0).astype(bf16)

    def spread(sub, carry):
        here = pl.ds(pl.multiple_of(sub * (TB * K_LOC), TB * K_LOC), TB * K_LOC)
        there = pl.ds(half * LANES + sub * TB, TB)
        rows = jnp.concatenate([ut[i, here, :] for i in range(2)], axis=1).astype(bf16)
        for pair in range(B // 4):
            moved = [
                jnp.dot(rows, shift[2 * pair + i], preferred_element_type=f32).reshape(TB, K_LOC, 256)
                for i in range(2)
            ]
            both = jnp.concatenate(moved, axis=1).astype(bf16)
            toep[there, 16 * pair : 16 * pair + 16, :] = both
            both = pltpu.roll(both.reshape(TB * 16, 256), B // 2, 1).reshape(TB, 16, 256)
            toep[there, 64 + 16 * pair : 80 + 16 * pair, :] = both
        return carry

    lax.fori_loop(0, LANES // TB, spread, 0)


def units(templates, late):
    c_loc = templates.shape[2]
    return pl.pallas_call(
        unit_kernel,
        grid=(c_loc // LANES,),
        in_specs=[
            pl.BlockSpec((K_LOC, M, LANES), lambda h: (0, 0, h)),
            pl.BlockSpec((late.shape[0], LANES), lambda h: (0, h)),
        ],
        out_specs=[
            pl.BlockSpec(memory_space=pltpu.VMEM),
            pl.BlockSpec((K_LOC, LANES), lambda h: (0, h)),
            pl.BlockSpec((LANES, SLAB), lambda h: (h, 0)),
            pl.BlockSpec(memory_space=pltpu.VMEM),
            pl.BlockSpec(memory_space=pltpu.VMEM),
        ],
        out_shape=[
            jax.ShapeDtypeStruct((c_loc, K_LOC * B, 256), jnp.bfloat16),
            jax.ShapeDtypeStruct((K_LOC, c_loc), jnp.float32),
            jax.ShapeDtypeStruct((c_loc, SLAB), jnp.bfloat16),
            jax.ShapeDtypeStruct((1024, 256), jnp.bfloat16),
            jax.ShapeDtypeStruct((SLAB, SLAB), jnp.bfloat16),
        ],
        scratch_shapes=[
            pltpu.VMEM((2, LANES * K_LOC, LANES), jnp.float32),
            pltpu.VMEM((B // 2, 256, 256), jnp.bfloat16),
        ],
        compiler_params=pltpu.CompilerParams(vmem_limit_bytes=20 << 20),
        cost_estimate=pl.CostEstimate(flops=10**8, bytes_accessed=9 * 10**6, transcendentals=0),
        name="units",
    )(templates, late)


def lag_of(n):
    return B * ((n % B) ^ 7) + n // B


def swap_chunks(tiles, lane):
    for d in (4, 2, 1):
        upper = (lane // B) % (2 * d) >= d
        swapped = []
        for b in range(TA):
            other = tiles[b ^ d]
            if b & d:
                swapped.append(jnp.where(upper, tiles[b], pltpu.roll(other, LANES - B * d, 1)))
            else:
                swapped.append(jnp.where(upper, pltpu.roll(other, B * d, 1), tiles[b]))
        tiles = swapped
    return tiles


def correlate_kernel(place_ref, *refs):
    slabs = refs[:TA]
    tail_ref, toep, usum_ref, band, to_lag, out_ref = refs[TA : TA + 6]
    xa, xb, high, low, s_scr, mu_s, acc = refs[TA + 6 :]
    step = pl.program_id(0)
    f32, bf16 = jnp.float32, jnp.bfloat16
    groups = CB // 8

    @pl.when(step == 0)
    def _():
        acc[...] = jnp.zeros_like(acc)

    def place(where, part):
        wide = part.astype(f32)
        square = wide * wide
        top = square.astype(bf16)
        xb[:, where] = part
        high[:, where] = top
        low[:, where] = (square - top.astype(f32)).astype(bf16)
        xa[:, :, where] = wide.reshape(groups, 8, SLAB)

    half, x = place_ref[0] // 4, place_ref[0] % 4
    for i in range(TA):
        slab = (half if i < 4 else 1 - half) * 4 + (x + 4 - i % 4) % 4
        place(pl.ds(pl.multiple_of(slab * SLAB, SLAB), SLAB), slabs[i][...])
    place(pl.ds(TA * SLAB, SLAB), tail_ref[...])

    dot = functools.partial(jnp.dot, preferred_element_type=f32)
    spans = [slice(SLAB * b, SLAB * b + 512) for b in range(TA)]
    s1 = dot(jnp.concatenate([xb[:, span] for span in spans], axis=0), band[:512])
    s2 = dot(
        jnp.concatenate(
            [jnp.concatenate([high[:, span], low[:, span]], axis=1) for span in spans], axis=0
        ),
        band[...],
    )
    scale = lax.rsqrt(jnp.maximum(s2 - s1 * s1 * (1.0 / M), 0.0) + M * 1e-6)
    smu = (s1 * scale).astype(bf16)
    channels = pl.ds(pl.multiple_of(step * CB, CB), CB)
    for b in range(TA):
        mu_s[channels, SLAB * b : SLAB * b + SLAB] = smu[CB * b : CB * b + CB]
    lane = lax.broadcasted_iota(jnp.int32, (8, LANES), 1)
    for g in range(groups):
        for h in range(2):
            tiles = [
                scale[CB * b + 8 * g : CB * b + 8 * g + 8, LANES * h : LANES * h + LANES]
                for b in range(TA)
            ]
            for i, tile in enumerate(swap_chunks(tiles, lane)):
                s_scr[g, 8 * h + i] = tile

    back = 7 - lax.broadcasted_iota(jnp.int32, (8, LANES), 0)
    inside = lane + B * back < LANES
    total = [acc[8 * i : 8 * i + 8, :] for i in range(B)]
    for g in range(groups):
        for cc in range(8):
            turned = []
            for q in range(TILES + 2):
                row = xa[g, cc : cc + 1, LANES * q : LANES * q + LANES]
                row = jnp.broadcast_to(row, (8, LANES))
                turned.append(pltpu.roll(row, B, 1, stride=B, stride_axis=0))
            tiles = [jnp.where(inside, turned[q], turned[q + 1]) for q in range(TILES + 1)]
            x0 = jnp.concatenate(tiles[:TILES], axis=0).astype(bf16)
            x1 = jnp.concatenate(tiles[1:], axis=0).astype(bf16)
            x = jnp.concatenate([x0, x1], axis=1)
            prod = lax.dot_general(
                toep[step * CB + g * 8 + cc], x, (((1,), (1,)), ((), ())), preferred_element_type=f32
            )
            for i in range(B):
                factor = jnp.broadcast_to(s_scr[g, i, cc : cc + 1, :], (8, LANES))
                total[i] = total[i] + prod[8 * i : 8 * i + 8, :] * factor
    for i in range(B):
        acc[8 * i : 8 * i + 8, :] = total[i]

    @pl.when(step == pl.num_programs(0) - 1)
    def _():
        usum = usum_ref[...] * (1.0 / M)
        uh = usum.astype(bf16)
        ul = (usum - uh.astype(f32)).astype(bf16)
        smu = mu_s[...]
        fix = dot(uh, smu) + dot(ul, smu)
        halves = []
        for h in range(2):
            cols = [SLAB * b + LANES * h for b in range(TA)]
            fixes = swap_chunks([fix[:, c : c + LANES] for c in cols], lane)
            rows = [acc[64 * h + 8 * i : 64 * h + 8 * i + 8, :] - fixes[i] for i in range(TA)]
            halves.append(jnp.concatenate(swap_chunks(rows, lane), axis=0))
        value = jnp.concatenate(halves, axis=1) * (1.0 / C)
        lag = to_lag[...]
        v1 = value.astype(bf16)
        rest = value - v1.astype(f32)
        v2 = rest.astype(bf16)
        v3 = (rest - v2.astype(f32)).astype(bf16)
        value = dot(v1, lag) + dot(v2, lag) + dot(v3, lag)
        for i in range(32):
            out_ref[i] = value[2 * i : 2 * i + 2, :]


def correlate(place, slabs, tail, toep, usum, band, to_lag):
    c_loc = tail.shape[0]
    slab_spec = pl.BlockSpec((CB, SLAB), lambda i, o: (i, 0))
    return pl.pallas_call(
        correlate_kernel,
        grid_spec=pltpu.PrefetchScalarGridSpec(
            num_scalar_prefetch=1,
            grid=(c_loc // CB,),
            in_specs=[slab_spec] * (TA + 1)
            + [
                pl.BlockSpec(memory_space=pltpu.VMEM),
                pl.BlockSpec((K_LOC, c_loc), lambda i, o: (0, 0)),
                pl.BlockSpec(memory_space=pltpu.VMEM),
                pl.BlockSpec(memory_space=pltpu.VMEM),
            ],
            out_specs=pl.BlockSpec((32, 2, SLAB), lambda i, o: (0, 0, 0)),
            scratch_shapes=[
                pltpu.VMEM((CB // 8, 8, (TA + 1) * SLAB), jnp.float32),
                pltpu.VMEM((CB, (TA + 1) * SLAB), jnp.bfloat16),
                pltpu.VMEM((CB, (TA + 1) * SLAB), jnp.bfloat16),
                pltpu.VMEM((CB, (TA + 1) * SLAB), jnp.bfloat16),
                pltpu.VMEM((CB // 8, B, 8, LANES), jnp.float32),
                pltpu.VMEM((c_loc, TA * SLAB), jnp.bfloat16),
                pltpu.VMEM((LANES, LANES), jnp.float32),
            ],
        ),
        out_shape=jax.ShapeDtypeStruct((32, 2, SLAB), jnp.float32),
        compiler_params=pltpu.CompilerParams(vmem_limit_bytes=24 << 20),
        cost_estimate=pl.CostEstimate(flops=4 * 10**9, bytes_accessed=20 * 10**6, transcendentals=0),
        name="correlate",
    )(place, *slabs, tail, toep, usum, band, to_lag)


def along_x(by):
    return [(i, i // 4 * 4 + (i + by) % 4) for i in range(TA)]


ACROSS_Z = [(i, (i + 4) % TA) for i in range(TA)]
TO_OWNER = [
    ((4 * j + p) * TA + a, (4 * a + p) * TA + j) for j in range(TA) for p in range(4) for a in range(TA)
]


def on_device(templates, record, record_tail):
    late = jnp.transpose(record_tail)
    own = centred(record, late)
    other = lax.ppermute(own, "ta", ACROSS_Z)
    slabs = [own] + [lax.ppermute(own, "ta", along_x(by)) for by in (1, 2, 3)]
    slabs += [
        other,
        lax.ppermute(other, "ta", along_x(1)),
        lax.ppermute(other, "ta", along_x(2)),
        lax.ppermute(other, "ta", along_x(3)),
    ]
    place = lax.axis_index("ta").astype(jnp.int32).reshape(1)
    toep, usum, tail, band, to_lag = units(templates, late)
    part = correlate(place, slabs, tail, toep, usum, band, to_lag)
    summed = jnp.sum(lax.all_to_all(part, "ch", 0, 0), axis=0)
    return lax.ppermute(summed, ("ch", "ta"), TO_OWNER)


def solution(mesh):
    return jax.shard_map(
        on_device,
        mesh=mesh,
        in_specs=(P("ta", None, "ch"), P("ch", "ta"), P("ch", None)),
        out_specs=P("ch", "ta"),
        check_vma=False,
    )
```

```python
import functools
import math

import jax
import jax.numpy as jnp
from jax import lax
from jax.experimental import pallas as pl
from jax.experimental.pallas import tpu as pltpu
from jax.sharding import PartitionSpec as P

C = 8192
M = 200
K_LOC = 8
B = 16
CB = 64
TB = 128
SLAB = 256
TA = 8
LANES = 128
TILES = 16


def centre_kernel(record_hbm, late_hbm, own_ref, tail_ref, record, late, sems):
    copies = [
        pltpu.make_async_copy(late_hbm, late, sems.at[0]),
        pltpu.make_async_copy(record_hbm, record, sems.at[1]),
    ]
    for copy in copies:
        copy.start()
    copies[0].wait()
    after = late[...]
    centre = jnp.sum(after, axis=0, keepdims=True) / after.shape[0]
    column = jnp.broadcast_to(centre, (LANES, centre.shape[1])).T
    fill = jnp.zeros((SLAB - after.shape[0], after.shape[1]), jnp.float32)
    tail_ref[...] = jnp.concatenate([after - centre, fill], axis=0).T.astype(jnp.bfloat16)
    copies[1].wait()
    for i in range(SLAB // LANES):
        span = slice(LANES * i, LANES * i + LANES)
        own_ref[:, span] = (record[:, span] - column).astype(jnp.bfloat16)


def centred(record, late):
    shape = jax.ShapeDtypeStruct(record.shape, jnp.bfloat16)
    return pl.pallas_call(
        centre_kernel,
        in_specs=[pl.BlockSpec(memory_space=pltpu.HBM)] * 2,
        out_specs=[pl.BlockSpec(memory_space=pltpu.VMEM)] * 2,
        out_shape=[shape, shape],
        scratch_shapes=[
            pltpu.VMEM(record.shape, jnp.float32),
            pltpu.VMEM(late.shape, jnp.float32),
            pltpu.SemaphoreType.DMA((2,)),
        ],
        name="centre",
    )(record, late)


def unit_kernel(t_ref, toep, sum_ref, band, to_lag, ut, shift):
    f32, bf16 = jnp.float32, jnp.bfloat16
    for k in range(K_LOC):
        v = t_ref[k].astype(f32)
        v = v - jnp.sum(v, axis=0, keepdims=True) / M
        var = jnp.sum(v * v, axis=0, keepdims=True) / M
        unit = (v * lax.rsqrt(var + 1e-6) / math.sqrt(M)).astype(bf16).astype(f32)
        sum_ref[k : k + 1, :] = jnp.sum(unit, axis=0, keepdims=True)
        padded = jnp.concatenate([unit, jnp.zeros((256 - M, LANES), f32)], axis=0)
        turned = padded.T
        for i in range(2):
            ut[i, pl.ds(k, LANES, stride=K_LOC), :] = turned[:, LANES * i : LANES * i + LANES]

    half = pl.program_id(0)

    @pl.when(half == 0)
    def _():
        ahead = lax.broadcasted_iota(jnp.int32, (256, 256), 1) - lax.broadcasted_iota(
            jnp.int32, (256, 256), 0
        )
        for t0 in range(B // 2):
            shift[t0] = jnp.where(ahead == t0, 1.0, 0.0).astype(bf16)
        j = lax.broadcasted_iota(jnp.int32, (512, 256), 0)
        t = lag_of(lax.broadcasted_iota(jnp.int32, (512, 256), 1))
        once = jnp.where((j >= t) & (j < t + M), 1.0, 0.0).astype(bf16)
        band[:512] = once
        band[512:] = once
        n = lax.broadcasted_iota(jnp.int32, (SLAB, SLAB), 0)
        t = lax.broadcasted_iota(jnp.int32, (SLAB, SLAB), 1)
        to_lag[...] = jnp.where(t == lag_of(n), 1.0, 0.0).astype(bf16)

    def spread(sub, carry):
        here = pl.ds(pl.multiple_of(sub * (TB * K_LOC), TB * K_LOC), TB * K_LOC)
        there = pl.ds(half * LANES + sub * TB, TB)
        rows = jnp.concatenate([ut[i, here, :] for i in range(2)], axis=1).astype(bf16)
        for pair in range(B // 4):
            moved = [
                jnp.dot(rows, shift[2 * pair + i], preferred_element_type=f32).reshape(TB, K_LOC, 256)
                for i in range(2)
            ]
            both = jnp.concatenate(moved, axis=1).astype(bf16)
            toep[there, 16 * pair : 16 * pair + 16, :] = both
            both = pltpu.roll(both.reshape(TB * 16, 256), B // 2, 1).reshape(TB, 16, 256)
            toep[there, 64 + 16 * pair : 80 + 16 * pair, :] = both
        return carry

    lax.fori_loop(0, LANES // TB, spread, 0)


def units(templates):
    c_loc = templates.shape[2]
    return pl.pallas_call(
        unit_kernel,
        grid=(c_loc // LANES,),
        in_specs=[
            pl.BlockSpec((K_LOC, M, LANES), lambda h: (0, 0, h)),
        ],
        out_specs=[
            pl.BlockSpec(memory_space=pltpu.VMEM),
            pl.BlockSpec((K_LOC, LANES), lambda h: (0, h)),
            pl.BlockSpec(memory_space=pltpu.VMEM),
            pl.BlockSpec(memory_space=pltpu.VMEM),
        ],
        out_shape=[
            jax.ShapeDtypeStruct((c_loc, K_LOC * B, 256), jnp.bfloat16),
            jax.ShapeDtypeStruct((K_LOC, c_loc), jnp.float32),
            jax.ShapeDtypeStruct((1024, 256), jnp.bfloat16),
            jax.ShapeDtypeStruct((SLAB, SLAB), jnp.bfloat16),
        ],
        scratch_shapes=[
            pltpu.VMEM((2, LANES * K_LOC, LANES), jnp.float32),
            pltpu.VMEM((B // 2, 256, 256), jnp.bfloat16),
        ],
        compiler_params=pltpu.CompilerParams(vmem_limit_bytes=20 << 20),
        cost_estimate=pl.CostEstimate(flops=10**8, bytes_accessed=9 * 10**6, transcendentals=0),
        name="units",
    )(templates)


def lag_of(n):
    return B * ((n % B) ^ 7) + n // B


def swap_chunks(tiles, lane):
    for d in (4, 2, 1):
        upper = (lane // B) % (2 * d) >= d
        swapped = []
        for b in range(TA):
            other = tiles[b ^ d]
            if b & d:
                swapped.append(jnp.where(upper, tiles[b], pltpu.roll(other, LANES - B * d, 1)))
            else:
                swapped.append(jnp.where(upper, pltpu.roll(other, B * d, 1), tiles[b]))
        tiles = swapped
    return tiles


def correlate_kernel(place_ref, *refs):
    slabs = refs[:TA]
    tail_ref, toep, usum_ref, band, to_lag, out_ref = refs[TA : TA + 6]
    xa, xb, high, low, s_scr, mu_s, acc = refs[TA + 6 :]
    step = pl.program_id(0)
    f32, bf16 = jnp.float32, jnp.bfloat16
    groups = CB // 8

    @pl.when(step == 0)
    def _():
        acc[...] = jnp.zeros_like(acc)

    def place(where, part):
        wide = part.astype(f32)
        square = wide * wide
        top = square.astype(bf16)
        xb[:, where] = part
        high[:, where] = top
        low[:, where] = (square - top.astype(f32)).astype(bf16)
        xa[:, :, where] = wide.reshape(groups, 8, SLAB)

    half, x = place_ref[0] // 4, place_ref[0] % 4
    for i in range(TA):
        slab = (half if i < 4 else 1 - half) * 4 + (x + 4 - i % 4) % 4
        place(pl.ds(pl.multiple_of(slab * SLAB, SLAB), SLAB), slabs[i][...])
    place(pl.ds(TA * SLAB, SLAB), tail_ref[...])

    dot = functools.partial(jnp.dot, preferred_element_type=f32)
    spans = [slice(SLAB * b, SLAB * b + 512) for b in range(TA)]
    s1 = dot(jnp.concatenate([xb[:, span] for span in spans], axis=0), band[:512])
    s2 = dot(
        jnp.concatenate(
            [jnp.concatenate([high[:, span], low[:, span]], axis=1) for span in spans], axis=0
        ),
        band[...],
    )
    scale = lax.rsqrt(jnp.maximum(s2 - s1 * s1 * (1.0 / M), 0.0) + M * 1e-6)
    smu = (s1 * scale).astype(bf16)
    channels = pl.ds(pl.multiple_of(step * CB, CB), CB)
    for b in range(TA):
        mu_s[channels, SLAB * b : SLAB * b + SLAB] = smu[CB * b : CB * b + CB]
    lane = lax.broadcasted_iota(jnp.int32, (8, LANES), 1)
    for g in range(groups):
        for h in range(2):
            tiles = [
                scale[CB * b + 8 * g : CB * b + 8 * g + 8, LANES * h : LANES * h + LANES]
                for b in range(TA)
            ]
            for i, tile in enumerate(swap_chunks(tiles, lane)):
                s_scr[g, 8 * h + i] = tile

    back = 7 - lax.broadcasted_iota(jnp.int32, (8, LANES), 0)
    inside = lane + B * back < LANES
    total = [acc[8 * i : 8 * i + 8, :] for i in range(B)]
    for g in range(groups):
        for cc in range(8):
            turned = []
            for q in range(TILES + 2):
                row = xa[g, cc : cc + 1, LANES * q : LANES * q + LANES]
                row = jnp.broadcast_to(row, (8, LANES))
                turned.append(pltpu.roll(row, B, 1, stride=B, stride_axis=0))
            tiles = [jnp.where(inside, turned[q], turned[q + 1]) for q in range(TILES + 1)]
            x0 = jnp.concatenate(tiles[:TILES], axis=0).astype(bf16)
            x1 = jnp.concatenate(tiles[1:], axis=0).astype(bf16)
            x = jnp.concatenate([x0, x1], axis=1)
            prod = lax.dot_general(
                toep[step * CB + g * 8 + cc], x, (((1,), (1,)), ((), ())), preferred_element_type=f32
            )
            for i in range(B):
                factor = jnp.broadcast_to(s_scr[g, i, cc : cc + 1, :], (8, LANES))
                total[i] = total[i] + prod[8 * i : 8 * i + 8, :] * factor
    for i in range(B):
        acc[8 * i : 8 * i + 8, :] = total[i]

    @pl.when(step == pl.num_programs(0) - 1)
    def _():
        usum = usum_ref[...] * (1.0 / M)
        uh = usum.astype(bf16)
        ul = (usum - uh.astype(f32)).astype(bf16)
        smu = mu_s[...]
        fix = dot(uh, smu) + dot(ul, smu)
        halves = []
        for h in range(2):
            cols = [SLAB * b + LANES * h for b in range(TA)]
            fixes = swap_chunks([fix[:, c : c + LANES] for c in cols], lane)
            rows = [acc[64 * h + 8 * i : 64 * h + 8 * i + 8, :] - fixes[i] for i in range(TA)]
            halves.append(jnp.concatenate(swap_chunks(rows, lane), axis=0))
        value = jnp.concatenate(halves, axis=1) * (1.0 / C)
        lag = to_lag[...]
        v1 = value.astype(bf16)
        rest = value - v1.astype(f32)
        v2 = rest.astype(bf16)
        v3 = (rest - v2.astype(f32)).astype(bf16)
        value = dot(v1, lag) + dot(v2, lag) + dot(v3, lag)
        for i in range(32):
            out_ref[i] = value[2 * i : 2 * i + 2, :]


def correlate(place, slabs, tail, toep, usum, band, to_lag):
    c_loc = tail.shape[0]
    slab_spec = pl.BlockSpec((CB, SLAB), lambda i, o: (i, 0))
    return pl.pallas_call(
        correlate_kernel,
        grid_spec=pltpu.PrefetchScalarGridSpec(
            num_scalar_prefetch=1,
            grid=(c_loc // CB,),
            in_specs=[slab_spec] * (TA + 1)
            + [
                pl.BlockSpec(memory_space=pltpu.VMEM),
                pl.BlockSpec((K_LOC, c_loc), lambda i, o: (0, 0)),
                pl.BlockSpec(memory_space=pltpu.VMEM),
                pl.BlockSpec(memory_space=pltpu.VMEM),
            ],
            out_specs=pl.BlockSpec((32, 2, SLAB), lambda i, o: (0, 0, 0)),
            scratch_shapes=[
                pltpu.VMEM((CB // 8, 8, (TA + 1) * SLAB), jnp.float32),
                pltpu.VMEM((CB, (TA + 1) * SLAB), jnp.bfloat16),
                pltpu.VMEM((CB, (TA + 1) * SLAB), jnp.bfloat16),
                pltpu.VMEM((CB, (TA + 1) * SLAB), jnp.bfloat16),
                pltpu.VMEM((CB // 8, B, 8, LANES), jnp.float32),
                pltpu.VMEM((c_loc, TA * SLAB), jnp.bfloat16),
                pltpu.VMEM((LANES, LANES), jnp.float32),
            ],
        ),
        out_shape=jax.ShapeDtypeStruct((32, 2, SLAB), jnp.float32),
        compiler_params=pltpu.CompilerParams(vmem_limit_bytes=24 << 20),
        cost_estimate=pl.CostEstimate(flops=4 * 10**9, bytes_accessed=20 * 10**6, transcendentals=0),
        name="correlate",
    )(place, *slabs, tail, toep, usum, band, to_lag)


def along_x(by):
    return [(i, i // 4 * 4 + (i + by) % 4) for i in range(TA)]


ACROSS_Z = [(i, (i + 4) % TA) for i in range(TA)]
TO_OWNER = [
    ((4 * j + p) * TA + a, (4 * a + p) * TA + j) for j in range(TA) for p in range(4) for a in range(TA)
]


def on_device(templates, record, record_tail):
    late = jnp.transpose(record_tail)
    own, tail = centred(record, late)
    other = lax.ppermute(own, "ta", ACROSS_Z)
    slabs = [own] + [lax.ppermute(own, "ta", along_x(by)) for by in (1, 2, 3)]
    slabs += [
        other,
        lax.ppermute(other, "ta", along_x(1)),
        lax.ppermute(other, "ta", along_x(2)),
        lax.ppermute(other, "ta", along_x(3)),
    ]
    place = lax.axis_index("ta").astype(jnp.int32).reshape(1)
    toep, usum, band, to_lag = units(templates)
    part = correlate(place, slabs, tail, toep, usum, band, to_lag)
    summed = jnp.sum(lax.all_to_all(part, "ch", 0, 0), axis=0)
    return lax.ppermute(summed, ("ch", "ta"), TO_OWNER)


def solution(mesh):
    return jax.shard_map(
        on_device,
        mesh=mesh,
        in_specs=(P("ta", None, "ch"), P("ch", "ta"), P("ch", None)),
        out_specs=P("ch", "ta"),
        check_vma=False,
    )
```

```python
import functools
import math

import jax
import jax.numpy as jnp
from jax import lax
from jax.experimental import pallas as pl
from jax.experimental.pallas import tpu as pltpu
from jax.sharding import PartitionSpec as P

C = 8192
M = 200
K_LOC = 8
B = 16
CB = 64
TB = 128
SLAB = 256
TA = 8
LANES = 128
TILES = 16


def centre_kernel(record_ref, late_ref, own_ref, tail_ref):
    after = late_ref[...]
    centre = jnp.sum(after, axis=0, keepdims=True) / after.shape[0]
    column = jnp.broadcast_to(centre, (LANES, centre.shape[1])).T
    for i in range(SLAB // LANES):
        span = slice(LANES * i, LANES * i + LANES)
        own_ref[:, span] = (record_ref[:, span] - column).astype(jnp.bfloat16)
    fill = jnp.zeros((SLAB - after.shape[0], after.shape[1]), jnp.float32)
    tail_ref[...] = jnp.concatenate([after - centre, fill], axis=0).T.astype(jnp.bfloat16)


def centred(record, late):
    shape = jax.ShapeDtypeStruct(record.shape, jnp.bfloat16)
    return pl.pallas_call(
        centre_kernel,
        in_specs=[pl.BlockSpec(memory_space=pltpu.VMEM)] * 2,
        out_specs=[pl.BlockSpec(memory_space=pltpu.VMEM)] * 2,
        out_shape=[shape, shape],
        compiler_params=pltpu.CompilerParams(vmem_limit_bytes=8 << 20),
        name="centre",
    )(record, late)


def unit_kernel(t_ref, toep, sum_ref, band, to_lag, ut, shift):
    f32, bf16 = jnp.float32, jnp.bfloat16
    for k in range(K_LOC):
        v = t_ref[k].astype(f32)
        v = v - jnp.sum(v, axis=0, keepdims=True) / M
        var = jnp.sum(v * v, axis=0, keepdims=True) / M
        unit = (v * lax.rsqrt(var + 1e-6) / math.sqrt(M)).astype(bf16).astype(f32)
        sum_ref[k : k + 1, :] = jnp.sum(unit, axis=0, keepdims=True)
        padded = jnp.concatenate([unit, jnp.zeros((256 - M, LANES), f32)], axis=0)
        turned = padded.T
        for i in range(2):
            ut[i, pl.ds(k, LANES, stride=K_LOC), :] = turned[:, LANES * i : LANES * i + LANES]

    half = pl.program_id(0)

    @pl.when(half == 0)
    def _():
        ahead = lax.broadcasted_iota(jnp.int32, (256, 256), 1) - lax.broadcasted_iota(
            jnp.int32, (256, 256), 0
        )
        for t0 in range(B // 2):
            shift[t0] = jnp.where(ahead == t0, 1.0, 0.0).astype(bf16)
        j = lax.broadcasted_iota(jnp.int32, (512, 256), 0)
        t = lag_of(lax.broadcasted_iota(jnp.int32, (512, 256), 1))
        once = jnp.where((j >= t) & (j < t + M), 1.0, 0.0).astype(bf16)
        band[:512] = once
        band[512:] = once
        n = lax.broadcasted_iota(jnp.int32, (SLAB, SLAB), 0)
        t = lax.broadcasted_iota(jnp.int32, (SLAB, SLAB), 1)
        to_lag[...] = jnp.where(t == lag_of(n), 1.0, 0.0).astype(bf16)

    def spread(sub, carry):
        here = pl.ds(pl.multiple_of(sub * (TB * K_LOC), TB * K_LOC), TB * K_LOC)
        there = pl.ds(half * LANES + sub * TB, TB)
        rows = jnp.concatenate([ut[i, here, :] for i in range(2)], axis=1).astype(bf16)
        for pair in range(B // 4):
            moved = [
                jnp.dot(rows, shift[2 * pair + i], preferred_element_type=f32).reshape(TB, K_LOC, 256)
                for i in range(2)
            ]
            both = jnp.concatenate(moved, axis=1).astype(bf16)
            toep[there, 16 * pair : 16 * pair + 16, :] = both
            both = pltpu.roll(both.reshape(TB * 16, 256), B // 2, 1).reshape(TB, 16, 256)
            toep[there, 64 + 16 * pair : 80 + 16 * pair, :] = both
        return carry

    lax.fori_loop(0, LANES // TB, spread, 0)


def units(templates):
    c_loc = templates.shape[2]
    return pl.pallas_call(
        unit_kernel,
        grid=(c_loc // LANES,),
        in_specs=[
            pl.BlockSpec((K_LOC, M, LANES), lambda h: (0, 0, h)),
        ],
        out_specs=[
            pl.BlockSpec(memory_space=pltpu.VMEM),
            pl.BlockSpec((K_LOC, LANES), lambda h: (0, h)),
            pl.BlockSpec(memory_space=pltpu.VMEM),
            pl.BlockSpec(memory_space=pltpu.VMEM),
        ],
        out_shape=[
            jax.ShapeDtypeStruct((c_loc, K_LOC * B, 256), jnp.bfloat16),
            jax.ShapeDtypeStruct((K_LOC, c_loc), jnp.float32),
            jax.ShapeDtypeStruct((1024, 256), jnp.bfloat16),
            jax.ShapeDtypeStruct((SLAB, SLAB), jnp.bfloat16),
        ],
        scratch_shapes=[
            pltpu.VMEM((2, LANES * K_LOC, LANES), jnp.float32),
            pltpu.VMEM((B // 2, 256, 256), jnp.bfloat16),
        ],
        compiler_params=pltpu.CompilerParams(vmem_limit_bytes=20 << 20),
        cost_estimate=pl.CostEstimate(flops=10**8, bytes_accessed=9 * 10**6, transcendentals=0),
        name="units",
    )(templates)


def lag_of(n):
    return B * ((n % B) ^ 7) + n // B


def swap_chunks(tiles, lane):
    for d in (4, 2, 1):
        upper = (lane // B) % (2 * d) >= d
        swapped = []
        for b in range(TA):
            other = tiles[b ^ d]
            if b & d:
                swapped.append(jnp.where(upper, tiles[b], pltpu.roll(other, LANES - B * d, 1)))
            else:
                swapped.append(jnp.where(upper, pltpu.roll(other, B * d, 1), tiles[b]))
        tiles = swapped
    return tiles


def correlate_kernel(place_ref, *refs):
    slabs = refs[:TA]
    tail_ref, toep, usum_ref, band, to_lag, out_ref = refs[TA : TA + 6]
    xa, xb, high, low, s_scr, mu_s, acc = refs[TA + 6 :]
    step = pl.program_id(0)
    f32, bf16 = jnp.float32, jnp.bfloat16
    groups = CB // 8

    @pl.when(step == 0)
    def _():
        acc[...] = jnp.zeros_like(acc)

    def place(where, part):
        wide = part.astype(f32)
        square = wide * wide
        top = square.astype(bf16)
        xb[:, where] = part
        high[:, where] = top
        low[:, where] = (square - top.astype(f32)).astype(bf16)
        xa[:, :, where] = wide.reshape(groups, 8, SLAB)

    half, x = place_ref[0] // 4, place_ref[0] % 4
    for i in range(TA):
        slab = (half if i < 4 else 1 - half) * 4 + (x + 4 - i % 4) % 4
        place(pl.ds(pl.multiple_of(slab * SLAB, SLAB), SLAB), slabs[i][...])
    place(pl.ds(TA * SLAB, SLAB), tail_ref[...])

    dot = functools.partial(jnp.dot, preferred_element_type=f32)
    spans = [slice(SLAB * b, SLAB * b + 512) for b in range(TA)]
    s1 = dot(jnp.concatenate([xb[:, span] for span in spans], axis=0), band[:512])
    s2 = dot(
        jnp.concatenate(
            [jnp.concatenate([high[:, span], low[:, span]], axis=1) for span in spans], axis=0
        ),
        band[...],
    )
    scale = lax.rsqrt(jnp.maximum(s2 - s1 * s1 * (1.0 / M), 0.0) + M * 1e-6)
    smu = (s1 * scale).astype(bf16)
    channels = pl.ds(pl.multiple_of(step * CB, CB), CB)
    for b in range(TA):
        mu_s[channels, SLAB * b : SLAB * b + SLAB] = smu[CB * b : CB * b + CB]
    lane = lax.broadcasted_iota(jnp.int32, (8, LANES), 1)
    for g in range(groups):
        for h in range(2):
            tiles = [
                scale[CB * b + 8 * g : CB * b + 8 * g + 8, LANES * h : LANES * h + LANES]
                for b in range(TA)
            ]
            for i, tile in enumerate(swap_chunks(tiles, lane)):
                s_scr[g, 8 * h + i] = tile

    back = 7 - lax.broadcasted_iota(jnp.int32, (8, LANES), 0)
    inside = lane + B * back < LANES
    total = [acc[8 * i : 8 * i + 8, :] for i in range(B)]
    for g in range(groups):
        for cc in range(8):
            turned = []
            for q in range(TILES + 2):
                row = xa[g, cc : cc + 1, LANES * q : LANES * q + LANES]
                row = jnp.broadcast_to(row, (8, LANES))
                turned.append(pltpu.roll(row, B, 1, stride=B, stride_axis=0))
            tiles = [jnp.where(inside, turned[q], turned[q + 1]) for q in range(TILES + 1)]
            x0 = jnp.concatenate(tiles[:TILES], axis=0).astype(bf16)
            x1 = jnp.concatenate(tiles[1:], axis=0).astype(bf16)
            x = jnp.concatenate([x0, x1], axis=1)
            prod = lax.dot_general(
                toep[step * CB + g * 8 + cc], x, (((1,), (1,)), ((), ())), preferred_element_type=f32
            )
            for i in range(B):
                factor = jnp.broadcast_to(s_scr[g, i, cc : cc + 1, :], (8, LANES))
                total[i] = total[i] + prod[8 * i : 8 * i + 8, :] * factor
    for i in range(B):
        acc[8 * i : 8 * i + 8, :] = total[i]

    @pl.when(step == pl.num_programs(0) - 1)
    def _():
        usum = usum_ref[...] * (1.0 / M)
        uh = usum.astype(bf16)
        ul = (usum - uh.astype(f32)).astype(bf16)
        smu = mu_s[...]
        fix = dot(uh, smu) + dot(ul, smu)
        halves = []
        for h in range(2):
            cols = [SLAB * b + LANES * h for b in range(TA)]
            fixes = swap_chunks([fix[:, c : c + LANES] for c in cols], lane)
            rows = [acc[64 * h + 8 * i : 64 * h + 8 * i + 8, :] - fixes[i] for i in range(TA)]
            halves.append(jnp.concatenate(swap_chunks(rows, lane), axis=0))
        value = jnp.concatenate(halves, axis=1) * (1.0 / C)
        lag = to_lag[...]
        v1 = value.astype(bf16)
        rest = value - v1.astype(f32)
        v2 = rest.astype(bf16)
        v3 = (rest - v2.astype(f32)).astype(bf16)
        value = dot(v1, lag) + dot(v2, lag) + dot(v3, lag)
        for i in range(32):
            out_ref[i] = value[2 * i : 2 * i + 2, :]


def correlate(place, slabs, tail, toep, usum, band, to_lag):
    c_loc = tail.shape[0]
    slab_spec = pl.BlockSpec((CB, SLAB), lambda i, o: (i, 0))
    return pl.pallas_call(
        correlate_kernel,
        grid_spec=pltpu.PrefetchScalarGridSpec(
            num_scalar_prefetch=1,
            grid=(c_loc // CB,),
            in_specs=[slab_spec] * (TA + 1)
            + [
                pl.BlockSpec(memory_space=pltpu.VMEM),
                pl.BlockSpec((K_LOC, c_loc), lambda i, o: (0, 0)),
                pl.BlockSpec(memory_space=pltpu.VMEM),
                pl.BlockSpec(memory_space=pltpu.VMEM),
            ],
            out_specs=pl.BlockSpec((32, 2, SLAB), lambda i, o: (0, 0, 0)),
            scratch_shapes=[
                pltpu.VMEM((CB // 8, 8, (TA + 1) * SLAB), jnp.float32),
                pltpu.VMEM((CB, (TA + 1) * SLAB), jnp.bfloat16),
                pltpu.VMEM((CB, (TA + 1) * SLAB), jnp.bfloat16),
                pltpu.VMEM((CB, (TA + 1) * SLAB), jnp.bfloat16),
                pltpu.VMEM((CB // 8, B, 8, LANES), jnp.float32),
                pltpu.VMEM((c_loc, TA * SLAB), jnp.bfloat16),
                pltpu.VMEM((LANES, LANES), jnp.float32),
            ],
        ),
        out_shape=jax.ShapeDtypeStruct((32, 2, SLAB), jnp.float32),
        compiler_params=pltpu.CompilerParams(vmem_limit_bytes=24 << 20),
        cost_estimate=pl.CostEstimate(flops=4 * 10**9, bytes_accessed=20 * 10**6, transcendentals=0),
        name="correlate",
    )(place, *slabs, tail, toep, usum, band, to_lag)


def along_x(by):
    return [(i, i // 4 * 4 + (i + by) % 4) for i in range(TA)]


ACROSS_Z = [(i, (i + 4) % TA) for i in range(TA)]
TO_OWNER = [
    ((4 * j + p) * TA + a, (4 * a + p) * TA + j) for j in range(TA) for p in range(4) for a in range(TA)
]


def on_device(templates, record, record_tail):
    late = jnp.transpose(record_tail)
    own, tail = centred(record, late)
    other = lax.ppermute(own, "ta", ACROSS_Z)
    slabs = [own] + [lax.ppermute(own, "ta", along_x(by)) for by in (1, 2, 3)]
    slabs += [
        other,
        lax.ppermute(other, "ta", along_x(1)),
        lax.ppermute(other, "ta", along_x(2)),
        lax.ppermute(other, "ta", along_x(3)),
    ]
    place = lax.axis_index("ta").astype(jnp.int32).reshape(1)
    toep, usum, band, to_lag = units(templates)
    part = correlate(place, slabs, tail, toep, usum, band, to_lag)
    summed = jnp.sum(lax.all_to_all(part, "ch", 0, 0), axis=0)
    return lax.ppermute(summed, ("ch", "ta"), TO_OWNER)


def solution(mesh):
    return jax.shard_map(
        on_device,
        mesh=mesh,
        in_specs=(P("ta", None, "ch"), P("ch", "ta"), P("ch", None)),
        out_specs=P("ch", "ta"),
        check_vma=False,
    )
```

```python
import functools
import math

import jax
import jax.numpy as jnp
from jax import lax
from jax.experimental import pallas as pl
from jax.experimental.pallas import tpu as pltpu
from jax.sharding import PartitionSpec as P

C = 8192
M = 200
K_LOC = 8
B = 16
CB = 128
TB = 128
SLAB = 256
TA = 8
LANES = 128
TILES = 16


def centre_kernel(record_ref, late_ref, own_ref, tail_ref):
    after = late_ref[...]
    centre = jnp.sum(after, axis=0, keepdims=True) / after.shape[0]
    column = jnp.broadcast_to(centre, (LANES, centre.shape[1])).T
    for i in range(SLAB // LANES):
        span = slice(LANES * i, LANES * i + LANES)
        own_ref[:, span] = (record_ref[:, span] - column).astype(jnp.bfloat16)
    fill = jnp.zeros((SLAB - after.shape[0], after.shape[1]), jnp.float32)
    tail_ref[...] = jnp.concatenate([after - centre, fill], axis=0).T.astype(jnp.bfloat16)


def centred(record, late):
    shape = jax.ShapeDtypeStruct(record.shape, jnp.bfloat16)
    return pl.pallas_call(
        centre_kernel,
        in_specs=[pl.BlockSpec(memory_space=pltpu.VMEM)] * 2,
        out_specs=[pl.BlockSpec(memory_space=pltpu.VMEM)] * 2,
        out_shape=[shape, shape],
        compiler_params=pltpu.CompilerParams(vmem_limit_bytes=8 << 20),
        name="centre",
    )(record, late)


def unit_kernel(t_ref, toep, sum_ref, band, to_lag, ut, shift):
    f32, bf16 = jnp.float32, jnp.bfloat16
    for k in range(K_LOC):
        v = t_ref[k].astype(f32)
        v = v - jnp.sum(v, axis=0, keepdims=True) / M
        var = jnp.sum(v * v, axis=0, keepdims=True) / M
        unit = (v * lax.rsqrt(var + 1e-6) / math.sqrt(M)).astype(bf16).astype(f32)
        sum_ref[k : k + 1, :] = jnp.sum(unit, axis=0, keepdims=True)
        padded = jnp.concatenate([unit, jnp.zeros((256 - M, LANES), f32)], axis=0)
        turned = padded.T
        for i in range(2):
            ut[i, pl.ds(k, LANES, stride=K_LOC), :] = turned[:, LANES * i : LANES * i + LANES]

    half = pl.program_id(0)

    @pl.when(half == 0)
    def _():
        ahead = lax.broadcasted_iota(jnp.int32, (256, 256), 1) - lax.broadcasted_iota(
            jnp.int32, (256, 256), 0
        )
        for t0 in range(B // 2):
            shift[t0] = jnp.where(ahead == t0, 1.0, 0.0).astype(bf16)
        j = lax.broadcasted_iota(jnp.int32, (512, 256), 0)
        t = lag_of(lax.broadcasted_iota(jnp.int32, (512, 256), 1))
        once = jnp.where((j >= t) & (j < t + M), 1.0, 0.0).astype(bf16)
        band[:512] = once
        band[512:] = once
        n = lax.broadcasted_iota(jnp.int32, (SLAB, SLAB), 0)
        t = lax.broadcasted_iota(jnp.int32, (SLAB, SLAB), 1)
        to_lag[...] = jnp.where(t == lag_of(n), 1.0, 0.0).astype(bf16)

    def spread(sub, carry):
        here = pl.ds(pl.multiple_of(sub * (TB * K_LOC), TB * K_LOC), TB * K_LOC)
        there = pl.ds(half * LANES + sub * TB, TB)
        rows = jnp.concatenate([ut[i, here, :] for i in range(2)], axis=1).astype(bf16)
        for pair in range(B // 4):
            moved = [
                jnp.dot(rows, shift[2 * pair + i], preferred_element_type=f32).reshape(TB, K_LOC, 256)
                for i in range(2)
            ]
            both = jnp.concatenate(moved, axis=1).astype(bf16)
            toep[there, 16 * pair : 16 * pair + 16, :] = both
            both = pltpu.roll(both.reshape(TB * 16, 256), B // 2, 1).reshape(TB, 16, 256)
            toep[there, 64 + 16 * pair : 80 + 16 * pair, :] = both
        return carry

    lax.fori_loop(0, LANES // TB, spread, 0)


def units(templates):
    c_loc = templates.shape[2]
    return pl.pallas_call(
        unit_kernel,
        grid=(c_loc // LANES,),
        in_specs=[
            pl.BlockSpec((K_LOC, M, LANES), lambda h: (0, 0, h)),
        ],
        out_specs=[
            pl.BlockSpec(memory_space=pltpu.VMEM),
            pl.BlockSpec((K_LOC, LANES), lambda h: (0, h)),
            pl.BlockSpec(memory_space=pltpu.VMEM),
            pl.BlockSpec(memory_space=pltpu.VMEM),
        ],
        out_shape=[
            jax.ShapeDtypeStruct((c_loc, K_LOC * B, 256), jnp.bfloat16),
            jax.ShapeDtypeStruct((K_LOC, c_loc), jnp.float32),
            jax.ShapeDtypeStruct((1024, 256), jnp.bfloat16),
            jax.ShapeDtypeStruct((SLAB, SLAB), jnp.bfloat16),
        ],
        scratch_shapes=[
            pltpu.VMEM((2, LANES * K_LOC, LANES), jnp.float32),
            pltpu.VMEM((B // 2, 256, 256), jnp.bfloat16),
        ],
        compiler_params=pltpu.CompilerParams(vmem_limit_bytes=20 << 20),
        cost_estimate=pl.CostEstimate(flops=10**8, bytes_accessed=9 * 10**6, transcendentals=0),
        name="units",
    )(templates)


def lag_of(n):
    return B * ((n % B) ^ 7) + n // B


def swap_chunks(tiles, lane):
    for d in (4, 2, 1):
        upper = (lane // B) % (2 * d) >= d
        swapped = []
        for b in range(TA):
            other = tiles[b ^ d]
            if b & d:
                swapped.append(jnp.where(upper, tiles[b], pltpu.roll(other, LANES - B * d, 1)))
            else:
                swapped.append(jnp.where(upper, pltpu.roll(other, B * d, 1), tiles[b]))
        tiles = swapped
    return tiles


def correlate_kernel(place_ref, *refs):
    slabs = refs[:TA]
    tail_ref, toep, usum_ref, band, to_lag, out_ref = refs[TA : TA + 6]
    xa, xb, high, low, s_scr, mu_s, acc = refs[TA + 6 :]
    step = pl.program_id(0)
    f32, bf16 = jnp.float32, jnp.bfloat16
    groups = CB // 8

    @pl.when(step == 0)
    def _():
        acc[...] = jnp.zeros_like(acc)

    def place(where, part):
        wide = part.astype(f32)
        square = wide * wide
        top = square.astype(bf16)
        xb[:, where] = part
        high[:, where] = top
        low[:, where] = (square - top.astype(f32)).astype(bf16)
        xa[:, :, where] = wide.reshape(groups, 8, SLAB)

    half, x = place_ref[0] // 4, place_ref[0] % 4
    for i in range(TA):
        slab = (half if i < 4 else 1 - half) * 4 + (x + 4 - i % 4) % 4
        place(pl.ds(pl.multiple_of(slab * SLAB, SLAB), SLAB), slabs[i][...])
    place(pl.ds(TA * SLAB, SLAB), tail_ref[...])

    dot = functools.partial(jnp.dot, preferred_element_type=f32)
    spans = [slice(SLAB * b, SLAB * b + 512) for b in range(TA)]
    s1 = dot(jnp.concatenate([xb[:, span] for span in spans], axis=0), band[:512])
    s2 = dot(
        jnp.concatenate(
            [jnp.concatenate([high[:, span], low[:, span]], axis=1) for span in spans], axis=0
        ),
        band[...],
    )
    scale = lax.rsqrt(jnp.maximum(s2 - s1 * s1 * (1.0 / M), 0.0) + M * 1e-6)
    smu = (s1 * scale).astype(bf16)
    channels = pl.ds(pl.multiple_of(step * CB, CB), CB)
    for b in range(TA):
        mu_s[channels, SLAB * b : SLAB * b + SLAB] = smu[CB * b : CB * b + CB]
    lane = lax.broadcasted_iota(jnp.int32, (8, LANES), 1)
    for g in range(groups):
        for h in range(2):
            tiles = [
                scale[CB * b + 8 * g : CB * b + 8 * g + 8, LANES * h : LANES * h + LANES]
                for b in range(TA)
            ]
            for i, tile in enumerate(swap_chunks(tiles, lane)):
                s_scr[g, 8 * h + i] = tile

    back = 7 - lax.broadcasted_iota(jnp.int32, (8, LANES), 0)
    inside = lane + B * back < LANES
    total = [acc[8 * i : 8 * i + 8, :] for i in range(B)]
    for g in range(groups):
        for cc in range(8):
            turned = []
            for q in range(TILES + 2):
                row = xa[g, cc : cc + 1, LANES * q : LANES * q + LANES]
                row = jnp.broadcast_to(row, (8, LANES))
                turned.append(pltpu.roll(row, B, 1, stride=B, stride_axis=0))
            tiles = [jnp.where(inside, turned[q], turned[q + 1]) for q in range(TILES + 1)]
            x0 = jnp.concatenate(tiles[:TILES], axis=0).astype(bf16)
            x1 = jnp.concatenate(tiles[1:], axis=0).astype(bf16)
            x = jnp.concatenate([x0, x1], axis=1)
            prod = lax.dot_general(
                toep[step * CB + g * 8 + cc], x, (((1,), (1,)), ((), ())), preferred_element_type=f32
            )
            for i in range(B):
                factor = jnp.broadcast_to(s_scr[g, i, cc : cc + 1, :], (8, LANES))
                total[i] = total[i] + prod[8 * i : 8 * i + 8, :] * factor
    for i in range(B):
        acc[8 * i : 8 * i + 8, :] = total[i]

    @pl.when(step == pl.num_programs(0) - 1)
    def _():
        usum = usum_ref[...] * (1.0 / M)
        uh = usum.astype(bf16)
        ul = (usum - uh.astype(f32)).astype(bf16)
        smu = mu_s[...]
        fix = dot(uh, smu) + dot(ul, smu)
        halves = []
        for h in range(2):
            cols = [SLAB * b + LANES * h for b in range(TA)]
            fixes = swap_chunks([fix[:, c : c + LANES] for c in cols], lane)
            rows = [acc[64 * h + 8 * i : 64 * h + 8 * i + 8, :] - fixes[i] for i in range(TA)]
            halves.append(jnp.concatenate(swap_chunks(rows, lane), axis=0))
        value = jnp.concatenate(halves, axis=1) * (1.0 / C)
        lag = to_lag[...]
        v1 = value.astype(bf16)
        rest = value - v1.astype(f32)
        v2 = rest.astype(bf16)
        v3 = (rest - v2.astype(f32)).astype(bf16)
        value = dot(v1, lag) + dot(v2, lag) + dot(v3, lag)
        for i in range(32):
            out_ref[i] = value[2 * i : 2 * i + 2, :]


def correlate(place, slabs, tail, toep, usum, band, to_lag):
    c_loc = tail.shape[0]
    slab_spec = pl.BlockSpec((CB, SLAB), lambda i, o: (i, 0))
    return pl.pallas_call(
        correlate_kernel,
        grid_spec=pltpu.PrefetchScalarGridSpec(
            num_scalar_prefetch=1,
            grid=(c_loc // CB,),
            in_specs=[slab_spec] * (TA + 1)
            + [
                pl.BlockSpec(memory_space=pltpu.VMEM),
                pl.BlockSpec((K_LOC, c_loc), lambda i, o: (0, 0)),
                pl.BlockSpec(memory_space=pltpu.VMEM),
                pl.BlockSpec(memory_space=pltpu.VMEM),
            ],
            out_specs=pl.BlockSpec((32, 2, SLAB), lambda i, o: (0, 0, 0)),
            scratch_shapes=[
                pltpu.VMEM((CB // 8, 8, (TA + 1) * SLAB), jnp.float32),
                pltpu.VMEM((CB, (TA + 1) * SLAB), jnp.bfloat16),
                pltpu.VMEM((CB, (TA + 1) * SLAB), jnp.bfloat16),
                pltpu.VMEM((CB, (TA + 1) * SLAB), jnp.bfloat16),
                pltpu.VMEM((CB // 8, B, 8, LANES), jnp.float32),
                pltpu.VMEM((c_loc, TA * SLAB), jnp.bfloat16),
                pltpu.VMEM((LANES, LANES), jnp.float32),
            ],
        ),
        out_shape=jax.ShapeDtypeStruct((32, 2, SLAB), jnp.float32),
        compiler_params=pltpu.CompilerParams(vmem_limit_bytes=24 << 20),
        cost_estimate=pl.CostEstimate(flops=4 * 10**9, bytes_accessed=20 * 10**6, transcendentals=0),
        name="correlate",
    )(place, *slabs, tail, toep, usum, band, to_lag)


def along_x(by):
    return [(i, i // 4 * 4 + (i + by) % 4) for i in range(TA)]


ACROSS_Z = [(i, (i + 4) % TA) for i in range(TA)]
TO_OWNER = [
    ((4 * j + p) * TA + a, (4 * a + p) * TA + j) for j in range(TA) for p in range(4) for a in range(TA)
]


def on_device(templates, record, record_tail):
    late = jnp.transpose(record_tail)
    own, tail = centred(record, late)
    other = lax.ppermute(own, "ta", ACROSS_Z)
    slabs = [own] + [lax.ppermute(own, "ta", along_x(by)) for by in (1, 2, 3)]
    slabs += [
        other,
        lax.ppermute(other, "ta", along_x(1)),
        lax.ppermute(other, "ta", along_x(2)),
        lax.ppermute(other, "ta", along_x(3)),
    ]
    place = lax.axis_index("ta").astype(jnp.int32).reshape(1)
    toep, usum, band, to_lag = units(templates)
    part = correlate(place, slabs, tail, toep, usum, band, to_lag)
    summed = jnp.sum(lax.all_to_all(part, "ch", 0, 0), axis=0)
    return lax.ppermute(summed, ("ch", "ta"), TO_OWNER)


def solution(mesh):
    return jax.shard_map(
        on_device,
        mesh=mesh,
        in_specs=(P("ta", None, "ch"), P("ch", "ta"), P("ch", None)),
        out_specs=P("ch", "ta"),
        check_vma=False,
    )
```
